128 devices in a mesh: tile: 16 (over z, x_hi, core), win: 8 (over y, x_lo).
Axes of the slice: x: 4 (x_hi: 2, x_lo: 2; x = x_hi * 2 + x_lo), y: 4, z: 4, core: 2. Of those that a mesh axis runs over, the one named last changes fastest.
Arguments:
- initial_state: float32 [8, 4, 8, 64, 2048], P('win', None, None, None, 'tile'), may hold values from -6 to 6
- observed: float32 [8, 4, 8, 64, 2048], P('win', None, None, None, 'tile'), may hold values from -6 to 6
- mixing: float32 [8, 64, 2048], P(None, None, 'tile'), may hold values from 0.02 to 0.2
- velocity: float32 [8, 64, 2048], P(None, None, 'tile'), may hold values from 0 to 0.15
- sea_mask: int32 [8, 64, 2048], P(None, None, 'tile'), may hold values 0 or 1
- partner: int32 [2048], P('tile'), may hold values from 0 to 2047, as said below
Outputs:
- state_gradient: float32 [8, 4, 8, 64, 2048], P('win', None, None, None, 'tile')
- mixing_gradient: float32 [8, 64, 2048], P(None, 'win', 'tile')
The draws below stay inside these ranges and needn't reach their ends.
Inputs may be any that keep to these rules, and one draw needn't show every extreme that they name: partner[i] = (s - i) mod 2048 for one whole number s of each draw, so that partner is its own inverse.
All inputs are finite; a program needn't handle non-finite values. No bound on the sum of `sea_mask` on one device may be relied on, other than what follows from the above.
Results may differ from the reference program's by a relative error of at most 0.00002.
Values sent between devices are 32-bit elements; how exact they have to be, the bound alone decides.
No kernel may reach another device: no remote copies, remote signals or barrier semaphores. Data moves between devices by JAX's collectives and lax.ppermute only.
A program may use at most 128 MiB of HBM per device.

```python
import math
import jax
import jax.numpy as jnp

TRACERS = 4
LEVELS = 8
LAT = 64
STEPS = 6
NLON = 2048
NWIN = 8
N_WIN = 8


def draw_partner(key, part):
    offset = jax.random.randint(key, (), 0, NLON, dtype=jnp.int32)
    places = jnp.arange(NLON, dtype=jnp.int32)
    return jnp.mod(offset - places, NLON).astype(jnp.int32)


def with_ends(drawn, own_key, least, top_value):
    spot = [jax.random.randint(jax.random.fold_in(own_key, axis), (), 0, length) for axis, length in enumerate(drawn.shape)]
    longest = drawn.shape.index(max(drawn.shape))
    beside = spot[:longest] + [(spot[longest] + 1) % drawn.shape[longest]] + spot[longest + 1:]
    return drawn.at[tuple(spot)].set(least).at[tuple(beside)].set(top_value)


def level_of(stream_key, dims, split, smallest, top_value):
    gain = 1.0
    for dim, parts in split:
        heights = jax.random.uniform(jax.random.fold_in(jax.random.fold_in(stream_key, 6), dim), (parts,), jnp.float32, smallest / len(split), top_value / len(split))
        gain = gain * jnp.repeat(jnp.exp(heights), dims[dim] // parts).reshape((-1,) + (1,) * (len(dims) - 1 - dim))
    return gain


def normal_values(key, dims, scale, most, split=(), held_as=jnp.bfloat16):
    result = jax.random.normal(key, dims, jnp.float32) * scale
    if len(split) > 0:
        result = level_of(key, dims, split, -0.22, 0.18) * result
    return jnp.clip(result, min=-most, max=most).astype(held_as)


def setup_inputs(seed: int = 0) -> dict:
    key_list = jax.random.split(jax.random.key(seed), 7)
    return {
        "initial_state": normal_values(key_list[0], (NWIN, TRACERS, LEVELS, LAT, NLON), 1.0, 6.0, ((0, 8), (4, 16)), jnp.float32),
        "observed": normal_values(key_list[1], (NWIN, TRACERS, LEVELS, LAT, NLON), 1.0, 6.0, ((0, 8), (4, 16)), jnp.float32),
        "mixing": jnp.clip(jnp.exp(math.log(0.2) - 2.3025851 * jax.random.uniform(key_list[2], (LEVELS, LAT, NLON), jnp.float32) ** level_of(key_list[2], (LEVELS, LAT, NLON), ((2, 16),), -0.2, 0.2)), 0.02, 0.2),
        "velocity": jnp.clip(0.15 * jax.random.uniform(key_list[3], (LEVELS, LAT, NLON), jnp.float32) ** level_of(key_list[3], (LEVELS, LAT, NLON), ((2, 16),), -0.2, 0.2), 0.0, 0.15),
        "sea_mask": with_ends((jax.random.randint(key_list[4], (LEVELS, LAT, NLON), 0, 8) < 7).astype(jnp.int32), jax.random.fold_in(key_list[4], 1), 0, 1),
        "partner": draw_partner(jax.random.fold_in(key_list[6], 71), 0),
    }


def north_south(field, ghost_row):
    north = jnp.concatenate([field[..., 1:, :], ghost_row[..., None, :]], axis=-2)
    south = jnp.concatenate([jnp.zeros_like(field[..., :1, :]), field[..., :-1, :]], axis=-2)
    return (north, south)

def advance(centre, east, west, north, south, mixing, velocity, wet, wet_east, wet_west, wet_north, wet_south):
    spread = wet_east * (east - centre) + wet_west * (west - centre) + wet_north * (north - centre) + wet_south * (south - centre)
    return centre + wet * (mixing * spread - velocity * wet_west * (centre - west))

def reference(initial_state, observed, mixing, velocity, sea_mask, partner):
    wet = sea_mask.astype(jnp.float32)
    wet_east = jnp.roll(wet, -1, axis=-1)
    wet_west = jnp.roll(wet, 1, axis=-1)
    wet_north, wet_south = north_south(wet, jnp.take(wet[:, -1, :], partner, axis=1))

    def run(start, coeff):
        field = start
        for moment in range(STEPS):
            ghost_row = jnp.take(field[:, :, -1, :], partner, axis=2)
            north, south = north_south(field, ghost_row)
            field = advance(field, jnp.roll(field, -1, axis=-1), jnp.roll(field, 1, axis=-1), north, south, coeff, velocity, wet, wet_east, wet_west, wet_north, wet_south)
        return field
    ends = [run(initial_state[window], mixing) for window in range(N_WIN)]
    mismatch = [jnp.zeros_like(ends[0])] + [initial_state[window] - ends[window - 1] for window in range(1, N_WIN)]
    grads = []
    mixing_sum = jnp.zeros_like(mixing)
    for window in range(N_WIN):
        forcing = wet * (ends[window] - observed[window])
        if window < N_WIN - 1:
            forcing = forcing - mismatch[window + 1]
        _, pullback = jax.vjp(run, initial_state[window], mixing)
        state_part, mixing_part = pullback(forcing)
        grads.append(state_part + mismatch[window])
        mixing_sum = mixing_sum + mixing_part
    return (jnp.stack(grads), mixing_sum)
```

```python
import functools

import jax
import jax.numpy as jnp
from jax import lax
from jax.experimental import pallas as pl
from jax.experimental.pallas import tpu as pltpu
from jax.sharding import PartitionSpec as P

STEPS = 6
TRACERS = 4
LEVELS = 8
LAT = 64
LANES = 128
NLON = 2048
TILES = NLON // LANES
WINDOWS = 8
HALO = STEPS
GHOST = 8
BLOCKS = (LAT + GHOST) // 8
PAD = 8
ROWS = PAD + LAT + GHOST + PAD
SEGMENT = 32
STRIP = TRACERS


def lane_of():
    return lax.broadcasted_iota(jnp.int32, (8, LANES), 1)


def placed(rows, first, lane):
    shift = (lane - first) % LANES
    return rows if shift == 0 else pltpu.roll(rows, shift, 1)


def within(lane, first, count=HALO):
    return (lane >= first) & (lane < first + count)


def edge_messages(fields, extras, lane):
    west = jnp.zeros((8, LANES), jnp.float32)
    east = west
    for t, rows in enumerate(fields):
        at = SEGMENT * t
        west = jnp.where(within(lane, at + 18), placed(rows, 0, at + 18), west)
        east = jnp.where(within(lane, at), placed(rows, LANES - HALO, at), east)
    for f, rows in enumerate(extras):
        at = SEGMENT * f + 24
        west = jnp.where(within(lane, at), placed(rows, 0, at), west)
        east = jnp.where(within(lane, at), placed(rows, LANES - HALO, at), east)
    return west, east


def strip_rows(fields, from_west, from_east, lane):
    place = lane % SEGMENT
    strip = jnp.where(place < 6, from_west, jnp.where(within(place, 18), from_east, 0.0))
    for t, rows in enumerate(fields):
        at = SEGMENT * t
        strip = jnp.where(within(lane, at + 6), placed(rows, 0, at + 6), strip)
        strip = jnp.where(within(lane, at + 12), placed(rows, LANES - HALO, at + 12), strip)
    return strip


def strip_extra(rows, f, from_west, from_east, lane):
    at = SEGMENT * f + 24
    strip = jnp.where(within(lane, 0), placed(from_west, at, 0), 0.0)
    strip = jnp.where(within(lane, 6), placed(rows, 0, 6), strip)
    strip = jnp.where(within(lane, 12), placed(rows, LANES - HALO, 12), strip)
    strip = jnp.where(within(lane, 18), placed(from_east, at, 18), strip)
    strip = strip + pltpu.roll(strip, SEGMENT, 1)
    return strip + pltpu.roll(strip, 2 * SEGMENT, 1)


def fold_places(offset, lane):
    place = lane % SEGMENT
    column = jnp.where(place < 12, place - HALO, place + 110)
    own = offset + 133 - lane
    strip = jnp.where(place < 24, offset + 133 - column, 0)
    return own, strip


def picked(blocks, at):
    index = at & (LANES - 1)
    block = at >> 7
    parts = [jnp.take_along_axis(rows, index, axis=1, mode="promise_in_bounds") for rows in blocks]
    return jnp.where(block == 0, parts[0], jnp.where(block == 1, parts[1], parts[2]))


def west_of(rows, strip, t, lane):
    return jnp.where(lane == 0, placed(strip, SEGMENT * t + 5, 0), pltpu.roll(rows, 1, 1))


def east_of(rows, strip, t, lane):
    return jnp.where(lane == LANES - 1, placed(strip, SEGMENT * t + 18, LANES - 1), pltpu.roll(rows, LANES - 1, 1))


def pack_kernel(init, mixing, velocity, mask, west, east, fold):
    lane = lane_of()
    for block in range(LAT // 8):
        rows = pl.ds(8 * block, 8)
        wet = mask[0, rows, :].astype(jnp.float32)
        fields = [wet * init[t, 0, rows, :] for t in range(TRACERS)]
        extras = [mixing[0, rows, :], velocity[0, rows, :], wet]
        west[0, rows, :], east[0, rows, :] = edge_messages(fields, extras, lane)
    for k in range(GHOST):
        row = pl.ds(LAT - 1 - k, 1)
        wet = mask[0, row, :].astype(jnp.float32)
        for t in range(TRACERS):
            fold[t, 0, pl.ds(k, 1), :] = wet * init[t, 0, row, :]
        fold[4, 0, pl.ds(k, 1), :] = mixing[0, row, :]
        fold[5, 0, pl.ds(k, 1), :] = velocity[0, row, :]
        fold[6, 0, pl.ds(k, 1), :] = wet


def forward_kernel(
    scalars, init, mixing, velocity, mask, from_west, from_east, fold0, fold1, fold2,
    ends, spreads, gain, inflow, keep, field, wets, counts, drifts,
):
    lane = lane_of()
    zero = jnp.zeros((PAD, LANES), jnp.float32)

    @pl.when(pl.program_id(0) == 0)
    def _():
        for plane in range(TRACERS + 1):
            for buffer in range(2):
                field[buffer, plane, pl.ds(0, PAD), :] = zero
                field[buffer, plane, pl.ds(ROWS - PAD, PAD), :] = zero
        for plane in range(2):
            wets[plane, pl.ds(0, PAD), :] = zero
            wets[plane, pl.ds(ROWS - PAD, PAD), :] = zero

    for block in range(LAT // 8):
        rows, to = pl.ds(8 * block, 8), pl.ds(PAD + 8 * block, 8)
        wet = mask[0, rows, :].astype(jnp.float32)
        west, east = from_west[0, rows, :], from_east[0, rows, :]
        fields = [wet * init[t, 0, rows, :] for t in range(TRACERS)]
        for t in range(TRACERS):
            field[0, t, to, :] = fields[t]
        field[0, STRIP, to, :] = strip_rows(fields, west, east, lane)
        mix, speed = mixing[0, rows, :], velocity[0, rows, :]
        gain[0, 0, rows, :] = mix
        inflow[0, 0, rows, :] = speed
        wets[0, to, :] = wet
        gain[1, 0, rows, :] = strip_extra(mix, 0, west, east, lane)
        inflow[1, 0, rows, :] = strip_extra(speed, 1, west, east, lane)
        wets[1, to, :] = strip_extra(wet, 2, west, east, lane)
    own, strip = fold_places(scalars[0], lane)
    rows, to = pl.ds(LAT, GHOST), pl.ds(PAD + LAT, GHOST)
    edges = zero
    for t in range(TRACERS):
        blocks = [fold[t, 0] for fold in (fold0, fold1, fold2)]
        field[0, t, to, :] = picked(blocks, own)
        edges = jnp.where(within(lane, SEGMENT * t, 24), picked(blocks, strip), edges)
    field[0, STRIP, to, :] = edges
    for f, (target, where) in enumerate(((gain, rows), (inflow, rows), (wets, to))):
        blocks = [fold[TRACERS + f, 0] for fold in (fold0, fold1, fold2)]
        index = (slice(None),) if target is wets else (0, slice(None))
        if target is wets:
            target[0, where, :] = picked(blocks, own)
            target[1, where, :] = picked(blocks, strip)
        else:
            target[0, 0, where, :] = picked(blocks, own)
            target[1, 0, where, :] = picked(blocks, strip)

    for block in range(BLOCKS):
        rows, start = pl.ds(8 * block, 8), PAD + 8 * block
        edge = wets[1, pl.ds(start, 8), :]
        for plane in range(2):
            wet = wets[plane, pl.ds(start, 8), :]
            north, south = wets[plane, pl.ds(start + 1, 8), :], wets[plane, pl.ds(start - 1, 8), :]
            if plane == 0:
                west, east = west_of(wet, edge, 0, lane), east_of(wet, edge, 0, lane)
            else:
                west, east = pltpu.roll(wet, 1, 1), pltpu.roll(wet, LANES - 1, 1)
            count = west + east + north + south
            spread = wet * gain[plane, 0, rows, :]
            carried = wet * inflow[plane, 0, rows, :]
            drift = carried * (west if block < LAT // 8 else east)
            counts[plane, rows, :] = count
            drifts[plane, rows, :] = drift
            gain[plane, 0, rows, :] = spread
            inflow[plane, 0, rows, :] = spread + carried
            keep[plane, 0, rows, :] = 1.0 - (count * spread + drift)

    def step(moment, carry):
        now = moment % 2
        later = 1 - now
        for block in range(BLOCKS):
            rows, start = pl.ds(8 * block, 8), PAD + 8 * block
            edge = field[now, STRIP, pl.ds(start, 8), :]
            for t in range(TRACERS + 1):
                plane = 1 if t == STRIP else 0
                centre = edge if t == STRIP else field[now, t, pl.ds(start, 8), :]
                north, south = field[now, t, pl.ds(start + 1, 8), :], field[now, t, pl.ds(start - 1, 8), :]
                if t == STRIP:
                    west, east = pltpu.roll(centre, 1, 1), pltpu.roll(centre, LANES - 1, 1)
                else:
                    west, east = west_of(centre, edge, t, lane), east_of(centre, edge, t, lane)
                spread = (west + east) + (north + south) - counts[plane, rows, :] * centre
                up = west if block < LAT // 8 else east
                if t < TRACERS and block < LAT // 8:
                    spreads[moment, t, 0, rows, :] = spread
                field[later, t, pl.ds(start, 8), :] = (
                    centre + gain[plane, 0, rows, :] * spread + drifts[plane, rows, :] * (up - centre)
                )
        return carry

    lax.fori_loop(0, STEPS, step, 0)
    for block in range(LAT // 8):
        rows = pl.ds(8 * block, 8)
        sea = mask[0, rows, :] > 0
        for t in range(TRACERS):
            ends[t, 0, rows, :] = jnp.where(sea, field[STEPS % 2, t, pl.ds(PAD + 8 * block, 8), :], init[t, 0, rows, :])


def forcing_kernel(scalars, ends, observed, following, mask, forcing, west, east, fold):
    lane = lane_of()
    onward = scalars[1].astype(jnp.float32)
    for block in range(LAT // 8):
        rows = pl.ds(8 * block, 8)
        wet = mask[0, rows, :].astype(jnp.float32)
        fields = []
        for t in range(TRACERS):
            end = ends[t, 0, rows, :]
            value = wet * ((end - observed[t, 0, rows, :]) + onward * (end - following[t, 0, rows, :]))
            forcing[t, 0, rows, :] = value
            fields.append(value)
        west[0, rows, :], east[0, rows, :] = edge_messages(fields, (), lane)
    for k in range(GHOST):
        for t in range(TRACERS):
            fold[t, 0, pl.ds(k, 1), :] = forcing[t, 0, pl.ds(LAT - 1 - k, 1), :]


def adjoint_kernel(
    scalars, forcing, from_west, from_east, fold0, fold1, fold2, gain, inflow, keep, spreads, init, following, mask,
    gradient, mixing_part, state, flux,
):
    lane = lane_of()
    zero = jnp.zeros((PAD, LANES), jnp.float32)
    onward = scalars[1].astype(jnp.float32)

    @pl.when(pl.program_id(0) == 0)
    def _():
        for plane in range(TRACERS + 1):
            for buffer in range(2):
                flux[buffer, plane, pl.ds(0, PAD), :] = zero
                flux[buffer, plane, pl.ds(ROWS - PAD, PAD), :] = zero

    def put(plane, block, value):
        rows, to = pl.ds(8 * block, 8), pl.ds(PAD + 8 * block, 8)
        state[plane, rows, :] = value
        flux[0, plane, to, :] = gain[1 if plane == STRIP else 0, 0, rows, :] * value

    for block in range(LAT // 8):
        rows = pl.ds(8 * block, 8)
        fields = [forcing[t, 0, rows, :] for t in range(TRACERS)]
        for t in range(TRACERS):
            put(t, block, fields[t])
        put(STRIP, block, strip_rows(fields, from_west[0, rows, :], from_east[0, rows, :], lane))
        mixing_part[block, 0] = zero
    own, strip = fold_places(scalars[0], lane)
    edges = zero
    for t in range(TRACERS):
        blocks = [fold[t, 0] for fold in (fold0, fold1, fold2)]
        put(t, LAT // 8, picked(blocks, own))
        edges = jnp.where(within(lane, SEGMENT * t, 24), picked(blocks, strip), edges)
    put(STRIP, LAT // 8, edges)

    def step(count, carry):
        moment = STEPS - 1 - count
        now = count % 2
        later = 1 - now
        for block in range(BLOCKS):
            rows, start = pl.ds(8 * block, 8), PAD + 8 * block
            edge = flux[now, STRIP, pl.ds(start, 8), :]
            edge_in = inflow[1, 0, rows, :] * state[STRIP, rows, :]
            total = mixing_part[block, 0] if block < LAT // 8 else None
            for t in range(TRACERS + 1):
                plane = 1 if t == STRIP else 0
                value = state[t, rows, :]
                passed = edge if t == STRIP else flux[now, t, pl.ds(start, 8), :]
                moved = edge_in if t == STRIP else inflow[0, 0, rows, :] * value
                north, south = flux[now, t, pl.ds(start + 1, 8), :], flux[now, t, pl.ds(start - 1, 8), :]
                from_left, from_right = (passed, moved) if block < LAT // 8 else (moved, passed)
                edge_left, edge_right = (edge, edge_in) if block < LAT // 8 else (edge_in, edge)
                if t == STRIP:
                    west, east = pltpu.roll(from_left, 1, 1), pltpu.roll(from_right, LANES - 1, 1)
                else:
                    west, east = west_of(from_left, edge_left, t, lane), east_of(from_right, edge_right, t, lane)
                if t < TRACERS and block < LAT // 8:
                    total = total + value * spreads[moment, t, 0, rows, :]
                value = keep[plane, 0, rows, :] * value + ((west + east) + (north + south))
                state[t, rows, :] = value
                flux[later, t, pl.ds(start, 8), :] = gain[plane, 0, rows, :] * value
            if block < LAT // 8:
                mixing_part[block, 0] = total
        return carry

    lax.fori_loop(0, STEPS, step, 0)
    for block in range(LAT // 8):
        rows = pl.ds(8 * block, 8)
        sea = mask[0, rows, :] > 0
        mixing_part[block, 0] = jnp.where(sea, mixing_part[block, 0], 0.0)
        for t in range(TRACERS):
            land = onward * (init[t, 0, rows, :] - following[t, 0, rows, :])
            gradient[t, 0, rows, :] = jnp.where(sea, state[t, rows, :], land)


def spec(shape, dim):
    block = tuple(1 if i == dim else n for i, n in enumerate(shape))
    return pl.BlockSpec(block, lambda level: tuple(level if i == dim else 0 for i in range(len(shape))))


FIELD = ((TRACERS, LEVELS, LAT, LANES), 1)
COEFFICIENT = ((LEVELS, LAT, LANES), 0)
PLANES = ((2, LEVELS, LAT + GHOST, LANES), 1)
SPREADS = ((STEPS, TRACERS, LEVELS, LAT, LANES), 2)
PARTS = ((LAT // 8, LEVELS, 8, LANES), 1)
SCALARS = pl.BlockSpec(memory_space=pltpu.SMEM)


def folded(count):
    return ((count, LEVELS, GHOST, LANES), 1)


def call(kernel, ins, outs, scratch=(), scalars=False, flops=0, name=None):
    bytes_accessed = 4 * sum(functools.reduce(lambda a, b: a * b, shape) for shape, _ in (*ins, *outs))
    return pl.pallas_call(
        kernel,
        grid=(LEVELS,),
        in_specs=([SCALARS] if scalars else []) + [spec(*one) for one in ins],
        out_specs=[spec(*one) for one in outs],
        out_shape=[jax.ShapeDtypeStruct(shape, jnp.float32) for shape, _ in outs],
        scratch_shapes=[pltpu.VMEM(shape, jnp.float32) for shape in scratch],
        cost_estimate=pl.CostEstimate(flops=flops, bytes_accessed=bytes_accessed, transcendentals=0),
        name=name,
    )


def passed_along(block, axis, distance):
    devices = range(lax.axis_size(axis))
    return lax.ppermute(block, axis, [(i - distance, i) for i in devices if i - distance in devices])


def around(block, steps):
    return lax.ppermute(block, "tile", [(i, (i + steps) % TILES) for i in range(TILES)])


def fold_exchange(case, rows):
    def branch(k):
        def exchange(rows):
            return tuple(lax.ppermute(rows, "tile", [(e, (k + j - e) % TILES) for e in range(TILES)]) for j in range(3))

        return exchange

    return lax.switch(case, [branch(k) for k in range(TILES)], rows)


def body(initial_state, observed, mixing, velocity, sea_mask, partner):
    start, target = initial_state[0], observed[0]
    window, tile = lax.axis_index("win"), lax.axis_index("tile")
    lowest = (partner[0] + LANES * tile - 133) % NLON
    case = lowest // LANES
    scalars = jnp.stack([lowest % LANES, (window < WINDOWS - 1).astype(jnp.int32)]).astype(jnp.int32)

    following = passed_along(start, "win", -1)
    west, east, fold = call(
        pack_kernel, [FIELD, COEFFICIENT, COEFFICIENT, COEFFICIENT], [COEFFICIENT, COEFFICIENT, folded(7)], name="pack"
    )(start, mixing, velocity, sea_mask)
    from_east, from_west = around(west, -1), around(east, 1)
    folds = fold_exchange(case, fold)
    ends, spreads, gain, inflow, keep = call(
        forward_kernel,
        [FIELD, COEFFICIENT, COEFFICIENT, COEFFICIENT, COEFFICIENT, COEFFICIENT] + [folded(7)] * 3,
        [FIELD, SPREADS, PLANES, PLANES, PLANES],
        scratch=[
            (2, TRACERS + 1, ROWS, LANES),
            (2, ROWS, LANES),
            (2, LAT + GHOST, LANES),
            (2, LAT + GHOST, LANES),
        ],
        scalars=True,
        flops=20_000_000,
        name="forward",
    )(scalars, start, mixing, velocity, sea_mask, from_west, from_east, *folds)
    forcing, west, east, fold = call(
        forcing_kernel,
        [FIELD, FIELD, FIELD, COEFFICIENT],
        [FIELD, COEFFICIENT, COEFFICIENT, folded(4)],
        scalars=True,
        name="forcing",
    )(scalars, ends, target, following, sea_mask)
    from_east, from_west = around(west, -1), around(east, 1)
    folds = fold_exchange(case, fold)
    previous = passed_along(ends, "win", 1)
    gradient, parts = call(
        adjoint_kernel,
        [FIELD, COEFFICIENT, COEFFICIENT] + [folded(4)] * 3 + [PLANES] * 3 + [SPREADS, FIELD, FIELD, COEFFICIENT],
        [FIELD, PARTS],
        scratch=[(TRACERS + 1, LAT + GHOST, LANES), (2, TRACERS + 1, ROWS, LANES)],
        scalars=True,
        flops=20_000_000,
        name="adjoint",
    )(scalars, forcing, from_west, from_east, *folds, gain, inflow, keep, spreads, start, following, sea_mask)
    mixing_gradient = lax.all_to_all(parts, "win", 0, 0, tiled=True).sum(axis=0)
    state_gradient = gradient + jnp.where(window > 0, start - previous, 0.0)
    return state_gradient[None], mixing_gradient


def solution(mesh):
    in_specs = (
        P("win", None, None, None, "tile"),
        P("win", None, None, None, "tile"),
        P(None, None, "tile"),
        P(None, None, "tile"),
        P(None, None, "tile"),
        P("tile"),
    )
    out_specs = (P("win", None, None, None, "tile"), P(None, "win", "tile"))
    return jax.shard_map(body, mesh=mesh, in_specs=in_specs, out_specs=out_specs, check_vma=False)
```

```python
import functools

import jax
import jax.numpy as jnp
from jax import lax
from jax.experimental import pallas as pl
from jax.experimental.pallas import tpu as pltpu
from jax.sharding import PartitionSpec as P

STEPS = 6
TRACERS = 4
LEVELS = 8
LAT = 64
LANES = 128
NLON = 2048
TILES = NLON // LANES
WINDOWS = 8
HALO = STEPS
GHOST = 8
BLOCKS = (LAT + GHOST) // 8
PAD = 8
ROWS = PAD + LAT + GHOST + PAD
PLANES = TRACERS + 1
STRIP = TRACERS
SEGMENT = 24
SPLIT = 116
THIRD = 117
SLOT = 16


def lanes(rows=8):
    return lax.broadcasted_iota(jnp.int32, (rows, LANES), 1)


def moved(rows, shift):
    if isinstance(shift, int):
        shift %= LANES
        if shift == 0:
            return rows
    return pltpu.roll(rows, shift, 1)


def within(lane, first, count):
    return (lane >= first) & (lane < first + count)


def edges_packed(fields, firsts, lane, out):
    west, east = out
    for rows, first in zip(fields, firsts, strict=True):
        here = within(lane, first, HALO)
        west = jnp.where(here, moved(rows, first), west)
        east = jnp.where(here, moved(rows, first + HALO), east)
    return west, east


def field_plane(rows, from_west, first, lane):
    return jnp.where(lane < HALO, moved(from_west, -first), moved(rows, HALO))


def strip_plane(fields, from_east, lane):
    strip = from_east
    for t, rows in enumerate(fields):
        strip = jnp.where(within(lane, SEGMENT * t, 18), moved(rows, SEGMENT * t - 110), strip)
    return jnp.where(lane < SEGMENT * TRACERS, strip, 0.0)


def spread_out(segment, lane):
    segment = jnp.where(lane < SEGMENT, segment, 0.0)
    segment = segment + moved(segment, SEGMENT)
    return segment + moved(segment, 2 * SEGMENT)


def fold_masks(offset):
    lane = lanes(HALO)
    plane = offset + 139 - ((lane + offset + 12) & (LANES - 1)) >= LANES
    strip = offset + 23 - ((lane + offset + 24) & (LANES - 1)) >= LANES
    return lane, plane, strip, lane + THIRD <= offset


def ghost_plane(first, second, third, slot, offset, masks):
    lane, plane, _, beyond = masks
    rows = moved(jnp.where(plane, second, first), (offset + 12) & (LANES - 1))
    return jnp.where(beyond, moved(third, (offset + LANES - SLOT * slot) & (LANES - 1)), rows)


def ghost_strip(first, second, t, offset, masks):
    return moved(jnp.where(masks[2], second, first), (offset + SEGMENT * (t + 1)) & (LANES - 1))


def own_columns(plane, strip, t, lane):
    return jnp.where(lane < SPLIT, moved(plane, -HALO), moved(strip, 110 - SEGMENT * t))


def fold_out(values, spare, lane, fold, third, level):
    few = jnp.zeros((8, LANES), jnp.float32)
    for f, rows in enumerate(values):
        back = jnp.take_along_axis(rows, LANES - 1 - lane, axis=1, mode="promise_in_bounds")
        spare[f] = back
        few = jnp.where(within(lane, SLOT * f, 12), moved(back, SLOT * f + 12), few)
    spare[len(values)] = few
    for k in range(HALO):
        for f in range(len(values)):
            fold[level, pl.ds(HALO * f + k, 1), :] = spare[f, pl.ds(7 - k, 1), :]
        third[level, pl.ds(k, 1), :] = spare[len(values), pl.ds(7 - k, 1), :]


def field_slots(group):
    return [SEGMENT * t + 18 - HALO * group for t in range(TRACERS)]


def extra_slots(group):
    return [SEGMENT * f + HALO * group for f in range(3)]


def each_block(count, unrolled, body):
    def several(i, carry):
        for j in range(unrolled):
            body(pl.multiple_of(8 * (unrolled * i + j), 8))
        return carry

    lax.fori_loop(0, count // unrolled, several, 0)


def pack_kernel(init, mixing, velocity, mask, west, east, fold, third, spare):
    lane = lanes()
    third[...] = jnp.zeros_like(third)

    def one_level(level, carry):
        for block in range(LAT // 16):
            out = (jnp.zeros((8, LANES), jnp.float32),) * 2
            for group in range(2):
                rows = pl.ds(8 * (block + LAT // 16 * group), 8)
                wet = mask[level, rows, :].astype(jnp.float32)
                values = [wet * init[t, level, rows, :] for t in range(TRACERS)]
                values += [mixing[level, rows, :], velocity[level, rows, :], wet]
                out = edges_packed(values, field_slots(group) + extra_slots(group), lane, out)
            west[level, pl.ds(8 * block, 8), :], east[level, pl.ds(8 * block, 8), :] = out
        fold_out(values, spare, lane, fold, third, level)
        return carry

    lax.fori_loop(0, mask.shape[0], one_level, 0)


def forward_kernel(
    scalars, init, mixing, velocity, mask, from_west, from_east, fold0, fold1, third,
    ends, spreads, gain, inflow, keep, even, odd, wets, counts, drifts,
):
    lane = lanes()
    zero = jnp.zeros((PAD, LANES), jnp.float32)

    @pl.when(pl.program_id(0) == 0)
    def _():
        for at in (pl.ds(0, PAD), pl.ds(PAD + LAT, GHOST), pl.ds(ROWS - PAD, PAD)):
            for plane in range(PLANES):
                even[plane, at, :] = zero
                odd[plane, at, :] = zero
            for plane in range(2):
                wets[plane, at, :] = zero
        for plane in range(2):
            counts[plane, pl.ds(LAT, GHOST), :] = zero
            drifts[plane, pl.ds(LAT, GHOST), :] = zero

    for group in range(2):

        def unfold(row, group=group):
            rows, to = pl.ds(LAT // 2 * group + row, 8), pl.ds(PAD + LAT // 2 * group + row, 8)
            wet = mask[0, rows, :].astype(jnp.float32)
            west, east = from_west[0, pl.ds(row, 8), :], from_east[0, pl.ds(row, 8), :]
            fields = [wet * init[t, 0, rows, :] for t in range(TRACERS)]
            for t, first in enumerate(field_slots(group)):
                even[t, to, :] = field_plane(fields[t], west, first, lane)
            even[STRIP, to, :] = strip_plane(fields, moved(east, HALO * group), lane)
            extras = ((mixing[0, rows, :], counts, rows), (velocity[0, rows, :], drifts, rows), (wet, wets, to))
            for (values, target, where), first in zip(extras, extra_slots(group), strict=True):
                target[0, where, :] = field_plane(values, west, first, lane)
                segment = jnp.where(lane < 18, moved(values, -110), moved(east, 18 - first))
                target[1, where, :] = spread_out(segment, lane)

        each_block(LAT // 16, 2, unfold)
    offset = scalars[0]
    masks = fold_masks(offset)
    narrow, few = masks[0], third[0, pl.ds(0, HALO), :]
    rows, to = pl.ds(LAT, HALO), pl.ds(PAD + LAT, HALO)
    strip = jnp.zeros((HALO, LANES), jnp.float32)
    for t in range(TRACERS):
        first, second = (fold[0, pl.ds(HALO * t, HALO), :] for fold in (fold0, fold1))
        even[t, to, :] = ghost_plane(first, second, few, t, offset, masks)
        strip = jnp.where(within(narrow, SEGMENT * t, SEGMENT), ghost_strip(first, second, t, offset, masks), strip)
    even[STRIP, to, :] = strip
    for slot, (target, where) in enumerate(((counts, rows), (drifts, rows), (wets, to)), TRACERS):
        first, second = (fold[0, pl.ds(HALO * slot, HALO), :] for fold in (fold0, fold1))
        target[0, where, :] = ghost_plane(first, second, few, slot, offset, masks)
        target[1, where, :] = spread_out(ghost_strip(first, second, 0, offset, masks), narrow)

    def coefficients(row, own=True):
        rows = pl.ds(row, 8)
        for plane in range(2):
            wet = wets[plane, pl.ds(PAD + row, 8), :]
            west, east = moved(wet, 1), moved(wet, -1)
            north, south = wets[plane, pl.ds(PAD + row + 1, 8), :], wets[plane, pl.ds(PAD + row - 1, 8), :]
            count = (west + east) + (north + south)
            spread = wet * counts[plane, rows, :]
            carried = wet * drifts[plane, rows, :]
            drift = carried * (west if own else east)
            counts[plane, rows, :] = count
            drifts[plane, rows, :] = drift
            gain[plane, 0, rows, :] = spread
            inflow[plane, 0, rows, :] = spread + carried
            keep[plane, 0, rows, :] = 1.0 - (count * spread + drift)

    each_block(LAT // 8, 4, coefficients)
    coefficients(LAT, own=False)

    def step(now, later, moment):
        for block in range(BLOCKS):
            rows, start = pl.ds(8 * block, 8), PAD + 8 * block
            for t in range(PLANES):
                plane = 1 if t == STRIP else 0
                centre = now[t, pl.ds(start, 8), :]
                west, east = moved(centre, 1), moved(centre, -1)
                spread = (west + east) + (now[t, pl.ds(start + 1, 8), :] + now[t, pl.ds(start - 1, 8), :])
                spread = spread - counts[plane, rows, :] * centre
                up = west if block < LAT // 8 else east
                if block < LAT // 8:
                    spreads[moment, t, 0, rows, :] = spread
                later[t, pl.ds(start, 8), :] = (
                    centre + gain[plane, 0, rows, :] * spread + drifts[plane, rows, :] * (up - centre)
                )

    def two_steps(pair, carry):
        step(even, odd, 2 * pair)
        step(odd, even, 2 * pair + 1)
        return carry

    lax.fori_loop(0, STEPS // 2, two_steps, 0)
    def own_ends(row):
        rows, at = pl.ds(row, 8), pl.ds(PAD + row, 8)
        sea = mask[0, rows, :] > 0
        strip = even[STRIP, at, :]
        for t in range(TRACERS):
            ends[t, 0, rows, :] = jnp.where(sea, own_columns(even[t, at, :], strip, t, lane), init[t, 0, rows, :])

    each_block(LAT // 8, 4, own_ends)


def forcing_kernel(scalars, ends, observed, following, mask, forcing, west, east, fold, third, spare):
    lane = lanes()
    onward = scalars[1].astype(jnp.float32)
    third[...] = jnp.zeros_like(third)

    def one_level(level, carry):
        for block in range(LAT // 32):
            out = (jnp.zeros((8, LANES), jnp.float32),) * 2
            for group in range(4):
                rows = pl.ds(8 * (block + LAT // 32 * group), 8)
                wet = mask[level, rows, :].astype(jnp.float32)
                values = []
                for t in range(TRACERS):
                    end = ends[t, level, rows, :]
                    ahead = onward * (end - following[t, level, rows, :])
                    values.append(wet * ((end - observed[t, level, rows, :]) + ahead))
                    forcing[t, level, rows, :] = values[t]
                out = edges_packed(values, field_slots(group), lane, out)
            west[level, pl.ds(8 * block, 8), :], east[level, pl.ds(8 * block, 8), :] = out
        fold_out(values, spare, lane, fold, third, level)
        return carry

    lax.fori_loop(0, mask.shape[0], one_level, 0)


def adjoint_kernel(
    scalars, forcing, from_west, from_east, fold0, fold1, third, gain, inflow, keep, spreads, init, following, mask,
    gradient, mixing_part, state, even, odd, sums,
):
    lane = lanes()
    zero = jnp.zeros((PAD, LANES), jnp.float32)
    onward = scalars[1].astype(jnp.float32)

    @pl.when(pl.program_id(0) == 0)
    def _():
        for plane in range(PLANES):
            state[plane, pl.ds(LAT, GHOST), :] = zero
            for at in (pl.ds(0, PAD), pl.ds(PAD + LAT, GHOST), pl.ds(ROWS - PAD, PAD)):
                even[plane, at, :] = zero
                odd[plane, at, :] = zero

    def put(plane, row, count, value):
        rows = pl.ds(row, count)
        state[plane, rows, :] = value
        even[plane, pl.ds(PAD + row, count), :] = gain[1 if plane == STRIP else 0, 0, rows, :] * value

    for block in range(LAT // 8):
        group, rows, packed = block // 2, pl.ds(8 * block, 8), pl.ds(8 * (block % 2), 8)
        west, east = from_west[0, packed, :], moved(from_east[0, packed, :], HALO * group)
        fields = [forcing[t, 0, rows, :] for t in range(TRACERS)]
        for t, first in enumerate(field_slots(group)):
            put(t, 8 * block, 8, field_plane(fields[t], west, first, lane))
        put(STRIP, 8 * block, 8, strip_plane(fields, east, lane))
        sums[0, rows, :] = zero
        sums[1, rows, :] = zero
    offset = scalars[0]
    masks = fold_masks(offset)
    narrow, few = masks[0], third[0, pl.ds(0, HALO), :]
    strip = jnp.zeros((HALO, LANES), jnp.float32)
    for t in range(TRACERS):
        first, second = (fold[0, pl.ds(HALO * t, HALO), :] for fold in (fold0, fold1))
        put(t, LAT, HALO, ghost_plane(first, second, few, t, offset, masks))
        strip = jnp.where(within(narrow, SEGMENT * t, SEGMENT), ghost_strip(first, second, t, offset, masks), strip)
    put(STRIP, LAT, HALO, strip)

    def step(now, later, moment):
        for block in range(BLOCKS):
            rows, start = pl.ds(8 * block, 8), PAD + 8 * block
            own = block < LAT // 8
            total = sums[0, rows, :] if own else None
            for t in range(PLANES):
                plane = 1 if t == STRIP else 0
                value = state[t, rows, :]
                passed = now[t, pl.ds(start, 8), :]
                carried = inflow[plane, 0, rows, :] * value
                west, east = (moved(passed, 1), moved(carried, -1)) if own else (moved(carried, 1), moved(passed, -1))
                around = (west + east) + (now[t, pl.ds(start + 1, 8), :] + now[t, pl.ds(start - 1, 8), :])
                if own:
                    product = value * spreads[moment, t, 0, rows, :]
                    if t == STRIP:
                        sums[1, rows, :] = sums[1, rows, :] + product
                    else:
                        total = total + product
                value = keep[plane, 0, rows, :] * value + around
                state[t, rows, :] = value
                later[t, pl.ds(start, 8), :] = gain[plane, 0, rows, :] * value
            if own:
                sums[0, rows, :] = total

    def two_steps(pair, carry):
        step(even, odd, STEPS - 1 - 2 * pair)
        step(odd, even, STEPS - 2 - 2 * pair)
        return carry

    lax.fori_loop(0, STEPS // 2, two_steps, 0)
    for block in range(LAT // 8):
        rows = pl.ds(8 * block, 8)
        sea = mask[0, rows, :] > 0
        strip, part = state[STRIP, rows, :], sums[1, rows, :]
        edge = moved(part, 110)
        for t in range(1, TRACERS):
            edge = edge + moved(part, 110 - SEGMENT * t)
        total = jnp.where(lane < SPLIT, moved(sums[0, rows, :], -HALO), edge)
        mixing_part[block, 0] = jnp.where(sea, total, 0.0)
        for t in range(TRACERS):
            land = onward * (init[t, 0, rows, :] - following[t, 0, rows, :])
            gradient[t, 0, rows, :] = jnp.where(sea, own_columns(state[t, rows, :], strip, t, lane), land)


def spec(shape, dim, count):
    block = tuple(count if i == dim else n for i, n in enumerate(shape))
    return pl.BlockSpec(block, lambda level: tuple(level if i == dim else 0 for i in range(len(shape))))


FIELD = ((TRACERS, LEVELS, LAT, LANES), 1)
COEFFICIENT = ((LEVELS, LAT, LANES), 0)
EDGES = ((LEVELS, LAT // 2, LANES), 0)
EDGES_FIELDS = ((LEVELS, LAT // 4, LANES), 0)
UNFOLDED = ((2, LEVELS, LAT + GHOST, LANES), 1)
SPREADS = ((STEPS, PLANES, LEVELS, LAT, LANES), 2)
PARTS = ((LAT // 8, LEVELS, 8, LANES), 1)
FOLD = ((LEVELS, (TRACERS + 3) * HALO, LANES), 0)
FOLD_FIELDS = ((LEVELS, TRACERS * HALO, LANES), 0)
FEW = ((LEVELS, 8, LANES), 0)
SCALARS = pl.BlockSpec(memory_space=pltpu.SMEM)


def call(kernel, ins, outs, scratch=(), scalars=False, flops=0, count=1, name=None):
    bytes_accessed = 4 * sum(functools.reduce(lambda a, b: a * b, shape) for shape, _ in (*ins, *outs))
    return pl.pallas_call(
        kernel,
        grid=(LEVELS // count,),
        in_specs=([SCALARS] if scalars else []) + [spec(*one, count) for one in ins],
        out_specs=[spec(*one, count) for one in outs],
        out_shape=[jax.ShapeDtypeStruct(shape, jnp.float32) for shape, _ in outs],
        scratch_shapes=[pltpu.VMEM(shape, jnp.float32) for shape in scratch],
        cost_estimate=pl.CostEstimate(flops=flops, bytes_accessed=bytes_accessed, transcendentals=0),
        name=name,
    )


def passed_along(block, axis, distance):
    devices = range(lax.axis_size(axis))
    return lax.ppermute(block, axis, [(i - distance, i) for i in devices if i - distance in devices])


def around(block, steps):
    return lax.ppermute(block, "tile", [(i, (i + steps) % TILES) for i in range(TILES)])


def folded(block, k):
    return lax.ppermute(block, "tile", [(e, (k - e) % TILES) for e in range(TILES)])


def fold_exchange(case, fold, third):
    def branch(k, three):
        def exchange(fold, third):
            few = folded(third, k + 2) if three else jnp.zeros_like(third)
            return folded(fold, k), folded(fold, k + 1), few

        return exchange

    return lax.switch(case, [branch(k, three) for three in (False, True) for k in range(TILES)], fold, third)


def body(initial_state, observed, mixing, velocity, sea_mask, partner):
    start, target = initial_state[0], observed[0]
    window, tile = lax.axis_index("win"), lax.axis_index("tile")
    lowest = (partner[0] + LANES * tile - 133) % NLON
    offset = lowest % LANES
    case = lowest // LANES + jnp.where(offset >= THIRD, TILES, 0)
    scalars = jnp.stack([offset, (window < WINDOWS - 1).astype(jnp.int32)]).astype(jnp.int32)

    following = passed_along(start, "win", -1)
    west, east, fold, third = call(
        pack_kernel,
        [FIELD, COEFFICIENT, COEFFICIENT, COEFFICIENT],
        [EDGES, EDGES, FOLD, FEW],
        scratch=[(TRACERS + 4, 8, LANES)],
        count=4,
        name="pack",
    )(start, mixing, velocity, sea_mask)
    from_east, from_west = around(west, -1), around(east, 1)
    folds = fold_exchange(case, fold, third)
    ends, spreads, gain, inflow, keep = call(
        forward_kernel,
        [FIELD, COEFFICIENT, COEFFICIENT, COEFFICIENT, EDGES, EDGES, FOLD, FOLD, FEW],
        [FIELD, SPREADS, UNFOLDED, UNFOLDED, UNFOLDED],
        scratch=[
            (PLANES, ROWS, LANES),
            (PLANES, ROWS, LANES),
            (2, ROWS, LANES),
            (2, LAT + GHOST, LANES),
            (2, LAT + GHOST, LANES),
        ],
        scalars=True,
        flops=20_000_000,
        name="forward",
    )(scalars, start, mixing, velocity, sea_mask, from_west, from_east, *folds)
    previous = passed_along(ends, "win", 1)
    forcing, west, east, fold, third = call(
        forcing_kernel,
        [FIELD, FIELD, FIELD, COEFFICIENT],
        [FIELD, EDGES_FIELDS, EDGES_FIELDS, FOLD_FIELDS, FEW],
        scratch=[(TRACERS + 1, 8, LANES)],
        scalars=True,
        count=4,
        name="forcing",
    )(scalars, ends, target, following, sea_mask)
    from_east, from_west = around(west, -1), around(east, 1)
    folds = fold_exchange(case, fold, third)
    gradient, parts = call(
        adjoint_kernel,
        [FIELD, EDGES_FIELDS, EDGES_FIELDS, FOLD_FIELDS, FOLD_FIELDS, FEW, UNFOLDED, UNFOLDED, UNFOLDED, SPREADS, FIELD, FIELD]
        + [COEFFICIENT],
        [FIELD, PARTS],
        scratch=[(PLANES, LAT + GHOST, LANES), (PLANES, ROWS, LANES), (PLANES, ROWS, LANES), (2, LAT, LANES)],
        scalars=True,
        flops=20_000_000,
        name="adjoint",
    )(scalars, forcing, from_west, from_east, *folds, gain, inflow, keep, spreads, start, following, sea_mask)
    mixing_gradient = lax.all_to_all(parts, "win", 0, 0, tiled=True).sum(axis=0)
    state_gradient = gradient + jnp.where(window > 0, start - previous, 0.0)
    return state_gradient[None], mixing_gradient


def solution(mesh):
    in_specs = (
        P("win", None, None, None, "tile"),
        P("win", None, None, None, "tile"),
        P(None, None, "tile"),
        P(None, None, "tile"),
        P(None, None, "tile"),
        P("tile"),
    )
    out_specs = (P("win", None, None, None, "tile"), P(None, "win", "tile"))
    return jax.shard_map(body, mesh=mesh, in_specs=in_specs, out_specs=out_specs, check_vma=False)
```

```python
import functools

import jax
import jax.numpy as jnp
from jax import lax
from jax.experimental import pallas as pl
from jax.experimental.pallas import tpu as pltpu
from jax.sharding import PartitionSpec as P

STEPS = 6
TRACERS = 4
LEVELS = 8
LAT = 64
LANES = 128
NLON = 2048
TILES = NLON // LANES
WINDOWS = 8
HALO = STEPS
GHOST = 8
BLOCKS = (LAT + GHOST) // 8
PAD = 8
ROWS = PAD + LAT + GHOST + PAD
PLANES = TRACERS + 1
STRIP = TRACERS
SEGMENT = 24
SPLIT = 116
THIRD = 117
SLOT = 16


def lanes(rows=8):
    return lax.broadcasted_iota(jnp.int32, (rows, LANES), 1)


def moved(rows, shift):
    if isinstance(shift, int):
        shift %= LANES
        if shift == 0:
            return rows
    return pltpu.roll(rows, shift, 1)


def within(lane, first, count):
    return (lane >= first) & (lane < first + count)


def edges_packed(fields, firsts, lane, out):
    west, east = out
    for rows, first in zip(fields, firsts, strict=True):
        here = within(lane, first, HALO)
        west = jnp.where(here, moved(rows, first), west)
        east = jnp.where(here, moved(rows, first + HALO), east)
    return west, east


def field_plane(rows, from_west, first, lane):
    return jnp.where(lane < HALO, moved(from_west, -first), moved(rows, HALO))


def strip_plane(fields, from_east, lane):
    strip = from_east
    for t, rows in enumerate(fields):
        strip = jnp.where(within(lane, SEGMENT * t, 18), moved(rows, SEGMENT * t - 110), strip)
    return jnp.where(lane < SEGMENT * TRACERS, strip, 0.0)


def spread_out(segment, lane):
    segment = jnp.where(lane < SEGMENT, segment, 0.0)
    segment = segment + moved(segment, SEGMENT)
    return segment + moved(segment, 2 * SEGMENT)


def fold_masks(offset):
    lane = lanes(HALO)
    plane = offset + 139 - ((lane + offset + 12) & (LANES - 1)) >= LANES
    strip = offset + 23 - ((lane + offset + 24) & (LANES - 1)) >= LANES
    return lane, plane, strip, lane + THIRD <= offset


def ghost_plane(first, second, third, slot, offset, masks):
    _, plane, _, beyond = masks
    rows = moved(jnp.where(plane, second, first), (offset + 12) & (LANES - 1))
    return jnp.where(beyond, moved(third, (offset + LANES - SLOT * slot) & (LANES - 1)), rows)


def ghost_strip(first, second, t, offset, masks):
    return moved(jnp.where(masks[2], second, first), (offset + SEGMENT * (t + 1)) & (LANES - 1))


def own_columns(plane, strip, t, lane):
    return jnp.where(lane < SPLIT, moved(plane, -HALO), moved(strip, 110 - SEGMENT * t))


def fold_out(values, spare, lane, fold, third, level):
    few = jnp.zeros((8, LANES), jnp.float32)
    for f, rows in enumerate(values):
        back = jnp.take_along_axis(rows, LANES - 1 - lane, axis=1, mode="promise_in_bounds")
        spare[f] = back
        few = jnp.where(within(lane, SLOT * f, 12), moved(back, SLOT * f + 12), few)
    spare[len(values)] = few
    for k in range(HALO):
        for f in range(len(values)):
            fold[level, pl.ds(HALO * f + k, 1), :] = spare[f, pl.ds(7 - k, 1), :]
        third[level, pl.ds(k, 1), :] = spare[len(values), pl.ds(7 - k, 1), :]


def field_slots(group):
    return [SEGMENT * t + 18 - HALO * group for t in range(TRACERS)]


def extra_slots(group):
    return [SEGMENT * f + HALO * group for f in range(3)]


def each_block(count, unrolled, body):
    def several(i, carry):
        for j in range(unrolled):
            body(pl.multiple_of(8 * (unrolled * i + j), 8))
        return carry

    lax.fori_loop(0, count // unrolled, several, 0)


def pack_kernel(init, mixing, velocity, mask, west, east, fold, third, spare):
    lane = lanes()
    third[...] = jnp.zeros_like(third)

    def one_level(level, carry):
        for block in range(LAT // 16):
            out = (jnp.zeros((8, LANES), jnp.float32),) * 2
            for group in range(2):
                rows = pl.ds(8 * (block + LAT // 16 * group), 8)
                wet = mask[level, rows, :].astype(jnp.float32)
                values = [wet * init[t, level, rows, :] for t in range(TRACERS)]
                values += [mixing[level, rows, :], velocity[level, rows, :], wet]
                out = edges_packed(values, field_slots(group) + extra_slots(group), lane, out)
            west[level, pl.ds(8 * block, 8), :], east[level, pl.ds(8 * block, 8), :] = out
        fold_out(values, spare, lane, fold, third, level)
        return carry

    lax.fori_loop(0, mask.shape[0], one_level, 0)


def forward_kernel(
    scalars, init, mixing, velocity, mask, from_west, from_east, fold0, fold1, third,
    ends_low, ends_high, spreads, gain, inflow, keep, even, odd, wets, counts, drifts,
):
    lane = lanes()
    zero = jnp.zeros((PAD, LANES), jnp.float32)

    @pl.when(pl.program_id(0) == 0)
    def _():
        for at in (pl.ds(0, PAD), pl.ds(PAD + LAT, GHOST), pl.ds(ROWS - PAD, PAD)):
            for plane in range(PLANES):
                even[plane, at, :] = zero
                odd[plane, at, :] = zero
            for plane in range(2):
                wets[plane, at, :] = zero
        for plane in range(2):
            counts[plane, pl.ds(LAT, GHOST), :] = zero
            drifts[plane, pl.ds(LAT, GHOST), :] = zero

    def unfold(row):
        west, east = from_west[0, pl.ds(row, 8), :], from_east[0, pl.ds(row, 8), :]
        for group in range(2):
            rows, to = pl.ds(LAT // 2 * group + row, 8), pl.ds(PAD + LAT // 2 * group + row, 8)
            wet = mask[0, rows, :].astype(jnp.float32)
            fields = [wet * init[t, 0, rows, :] for t in range(TRACERS)]
            for t, first in enumerate(field_slots(group)):
                even[t, to, :] = field_plane(fields[t], west, first, lane)
            even[STRIP, to, :] = strip_plane(fields, moved(east, HALO * group), lane)
            extras = ((mixing[0, rows, :], counts, rows), (velocity[0, rows, :], drifts, rows), (wet, wets, to))
            for (values, target, where), first in zip(extras, extra_slots(group), strict=True):
                target[0, where, :] = field_plane(values, west, first, lane)
                segment = jnp.where(lane < 18, moved(values, -110), moved(east, 18 - first))
                target[1, where, :] = spread_out(segment, lane)

    each_block(LAT // 16, 1, unfold)
    offset = scalars[0]
    masks = fold_masks(offset)
    narrow, few = masks[0], third[0, pl.ds(0, HALO), :]
    rows, to = pl.ds(LAT, HALO), pl.ds(PAD + LAT, HALO)
    strip = jnp.zeros((HALO, LANES), jnp.float32)
    for t in range(TRACERS):
        first, second = (fold[0, pl.ds(HALO * t, HALO), :] for fold in (fold0, fold1))
        even[t, to, :] = ghost_plane(first, second, few, t, offset, masks)
        strip = jnp.where(within(narrow, SEGMENT * t, SEGMENT), ghost_strip(first, second, t, offset, masks), strip)
    even[STRIP, to, :] = strip
    for slot, (target, where) in enumerate(((counts, rows), (drifts, rows), (wets, to)), TRACERS):
        first, second = (fold[0, pl.ds(HALO * slot, HALO), :] for fold in (fold0, fold1))
        target[0, where, :] = ghost_plane(first, second, few, slot, offset, masks)
        target[1, where, :] = spread_out(ghost_strip(first, second, 0, offset, masks), narrow)

    def coefficients(row, own=True):
        rows = pl.ds(row, 8)
        for plane in range(2):
            wet = wets[plane, pl.ds(PAD + row, 8), :]
            west, east = moved(wet, 1), moved(wet, -1)
            north, south = wets[plane, pl.ds(PAD + row + 1, 8), :], wets[plane, pl.ds(PAD + row - 1, 8), :]
            count = (west + east) + (north + south)
            spread = wet * counts[plane, rows, :]
            carried = wet * drifts[plane, rows, :]
            drift = carried * (west if own else east)
            counts[plane, rows, :] = count
            drifts[plane, rows, :] = drift
            gain[plane, 0, rows, :] = spread
            inflow[plane, 0, rows, :] = spread + carried
            keep[plane, 0, rows, :] = 1.0 - (count * spread + drift)

    each_block(LAT // 8, 4, coefficients)
    coefficients(LAT, own=False)

    def step(now, later, moment):
        for block in range(BLOCKS):
            rows, start = pl.ds(8 * block, 8), PAD + 8 * block
            for t in range(PLANES):
                plane = 1 if t == STRIP else 0
                centre = now[t, pl.ds(start, 8), :]
                west, east = moved(centre, 1), moved(centre, -1)
                spread = (west + east) + (now[t, pl.ds(start + 1, 8), :] + now[t, pl.ds(start - 1, 8), :])
                spread = spread - counts[plane, rows, :] * centre
                up = west if block < LAT // 8 else east
                if block < LAT // 8:
                    spreads[moment, t, 0, rows, :] = spread
                later[t, pl.ds(start, 8), :] = (
                    centre + gain[plane, 0, rows, :] * spread + drifts[plane, rows, :] * (up - centre)
                )

    def two_steps(pair, carry):
        step(even, odd, 2 * pair)
        step(odd, even, 2 * pair + 1)
        return carry

    lax.fori_loop(0, STEPS // 2, two_steps, 0)

    def own_ends(row):
        rows, at = pl.ds(row, 8), pl.ds(PAD + row, 8)
        sea = mask[0, rows, :] > 0
        strip = even[STRIP, at, :]
        for t in range(TRACERS):
            ends = (ends_low, ends_high)[t // 2]
            ends[t % 2, 0, rows, :] = jnp.where(sea, own_columns(even[t, at, :], strip, t, lane), init[t, 0, rows, :])

    each_block(LAT // 8, 2, own_ends)


def forcing_kernel(
    scalars, ends_low, ends_high, observed, next_low, next_high, mask, forcing, west, east, fold, third, spare
):
    lane = lanes()
    onward = scalars[1].astype(jnp.float32)
    third[...] = jnp.zeros_like(third)

    def one_level(level, carry):
        for block in range(LAT // 32):
            out = (jnp.zeros((8, LANES), jnp.float32),) * 2
            for group in range(4):
                rows = pl.ds(8 * (block + LAT // 32 * group), 8)
                wet = mask[level, rows, :].astype(jnp.float32)
                values = []
                for t in range(TRACERS):
                    end = (ends_low, ends_high)[t // 2][t % 2, level, rows, :]
                    ahead = onward * (end - (next_low, next_high)[t // 2][t % 2, level, rows, :])
                    values.append(wet * ((end - observed[t, level, rows, :]) + ahead))
                    forcing[t, level, rows, :] = values[t]
                out = edges_packed(values, field_slots(group), lane, out)
            west[level, pl.ds(8 * block, 8), :], east[level, pl.ds(8 * block, 8), :] = out
        fold_out(values, spare, lane, fold, third, level)
        return carry

    lax.fori_loop(0, mask.shape[0], one_level, 0)


def adjoint_kernel(
    scalars, forcing, from_west, from_east, fold0, fold1, third, gain, inflow, keep, spreads, init, next_low, next_high, mask,
    gradient, mixing_part, state, even, odd, sums,
):
    lane = lanes()
    zero = jnp.zeros((PAD, LANES), jnp.float32)
    onward = scalars[1].astype(jnp.float32)

    @pl.when(pl.program_id(0) == 0)
    def _():
        for plane in range(PLANES):
            state[plane, pl.ds(LAT, GHOST), :] = zero
            for at in (pl.ds(0, PAD), pl.ds(PAD + LAT, GHOST), pl.ds(ROWS - PAD, PAD)):
                even[plane, at, :] = zero
                odd[plane, at, :] = zero

    def put(plane, row, count, value):
        rows = pl.ds(row, count)
        state[plane, rows, :] = value
        even[plane, pl.ds(PAD + row, count), :] = gain[1 if plane == STRIP else 0, 0, rows, :] * value

    def unfold(row):
        west, east = from_west[0, pl.ds(row, 8), :], from_east[0, pl.ds(row, 8), :]
        for group in range(4):
            to = LAT // 4 * group + row
            rows = pl.ds(to, 8)
            fields = [forcing[t, 0, rows, :] for t in range(TRACERS)]
            for t, first in enumerate(field_slots(group)):
                put(t, to, 8, field_plane(fields[t], west, first, lane))
            put(STRIP, to, 8, strip_plane(fields, moved(east, HALO * group), lane))
            sums[0, rows, :] = zero
            sums[1, rows, :] = zero

    each_block(LAT // 32, 1, unfold)
    offset = scalars[0]
    masks = fold_masks(offset)
    narrow, few = masks[0], third[0, pl.ds(0, HALO), :]
    strip = jnp.zeros((HALO, LANES), jnp.float32)
    for t in range(TRACERS):
        first, second = (fold[0, pl.ds(HALO * t, HALO), :] for fold in (fold0, fold1))
        put(t, LAT, HALO, ghost_plane(first, second, few, t, offset, masks))
        strip = jnp.where(within(narrow, SEGMENT * t, SEGMENT), ghost_strip(first, second, t, offset, masks), strip)
    put(STRIP, LAT, HALO, strip)

    def step(now, later, moment):
        for block in range(BLOCKS):
            rows, start = pl.ds(8 * block, 8), PAD + 8 * block
            own = block < LAT // 8
            total = sums[0, rows, :] if own else None
            for t in range(PLANES):
                plane = 1 if t == STRIP else 0
                value = state[t, rows, :]
                passed = now[t, pl.ds(start, 8), :]
                carried = inflow[plane, 0, rows, :] * value
                west, east = (moved(passed, 1), moved(carried, -1)) if own else (moved(carried, 1), moved(passed, -1))
                around = (west + east) + (now[t, pl.ds(start + 1, 8), :] + now[t, pl.ds(start - 1, 8), :])
                if own:
                    product = value * spreads[moment, t, 0, rows, :]
                    if t == STRIP:
                        sums[1, rows, :] = sums[1, rows, :] + product
                    else:
                        total = total + product
                value = keep[plane, 0, rows, :] * value + around
                state[t, rows, :] = value
                later[t, pl.ds(start, 8), :] = gain[plane, 0, rows, :] * value
            if own:
                sums[0, rows, :] = total

    def two_steps(pair, carry):
        step(even, odd, STEPS - 1 - 2 * pair)
        step(odd, even, STEPS - 2 - 2 * pair)
        return carry

    lax.fori_loop(0, STEPS // 2, two_steps, 0)

    def own_results(row):
        rows = pl.ds(row, 8)
        sea = mask[0, rows, :] > 0
        strip, part = state[STRIP, rows, :], sums[1, rows, :]
        edge = moved(part, 110)
        for t in range(1, TRACERS):
            edge = edge + moved(part, 110 - SEGMENT * t)
        total = jnp.where(lane < SPLIT, moved(sums[0, rows, :], -HALO), edge)
        mixing_part[row // 8, 0] = jnp.where(sea, total, 0.0)
        for t in range(TRACERS):
            land = onward * (init[t, 0, rows, :] - (next_low, next_high)[t // 2][t % 2, 0, rows, :])
            gradient[t, 0, rows, :] = jnp.where(sea, own_columns(state[t, rows, :], strip, t, lane), land)

    each_block(LAT // 8, 2, own_results)


def spec(shape, dim, count):
    block = tuple(count if i == dim else n for i, n in enumerate(shape))
    return pl.BlockSpec(block, lambda level: tuple(level if i == dim else 0 for i in range(len(shape))))


FIELD = ((TRACERS, LEVELS, LAT, LANES), 1)
PAIR = ((TRACERS // 2, LEVELS, LAT, LANES), 1)
COEFFICIENT = ((LEVELS, LAT, LANES), 0)
EDGES = ((LEVELS, LAT // 2, LANES), 0)
EDGES_FIELDS = ((LEVELS, LAT // 4, LANES), 0)
UNFOLDED = ((2, LEVELS, LAT + GHOST, LANES), 1)
SPREADS = ((STEPS, PLANES, LEVELS, LAT, LANES), 2)
PARTS = ((LAT // 8, LEVELS, 8, LANES), 1)
FOLD = ((LEVELS, (TRACERS + 3) * HALO, LANES), 0)
FOLD_FIELDS = ((LEVELS, TRACERS * HALO, LANES), 0)
FEW = ((LEVELS, 8, LANES), 0)
SCALARS = pl.BlockSpec(memory_space=pltpu.SMEM)


def call(kernel, ins, outs, scratch=(), scalars=False, flops=0, count=1):
    bytes_accessed = 4 * sum(functools.reduce(lambda a, b: a * b, shape) for shape, _ in (*ins, *outs))
    return pl.pallas_call(
        kernel,
        grid=(LEVELS // count,),
        in_specs=([SCALARS] if scalars else []) + [spec(*one, count) for one in ins],
        out_specs=[spec(*one, count) for one in outs],
        out_shape=[jax.ShapeDtypeStruct(shape, jnp.float32) for shape, _ in outs],
        scratch_shapes=[pltpu.VMEM(shape, jnp.float32) for shape in scratch],
        cost_estimate=pl.CostEstimate(flops=flops, bytes_accessed=bytes_accessed, transcendentals=0),
        compiler_params=pltpu.CompilerParams(vmem_limit_bytes=67_000_000),
    )


def passed_along(block, distance):
    return lax.ppermute(block, "win", [(i - distance, i) for i in range(WINDOWS) if i - distance in range(WINDOWS)])


def around(block, steps):
    return lax.ppermute(block, "tile", [(i, (i + steps) % TILES) for i in range(TILES)])


def folded(block, k):
    return lax.ppermute(block, "tile", [(e, (k - e) % TILES) for e in range(TILES)])


def fold_exchange(case, fold, third):
    def branch(k, three):
        def exchange(fold, third):
            few = folded(third, k + 2) if three else jnp.zeros_like(third)
            return folded(fold, k), folded(fold, k + 1), few

        return exchange

    return lax.switch(case, [branch(k, three) for three in (False, True) for k in range(TILES)], fold, third)


def body(initial_state, observed, mixing, velocity, sea_mask, partner):
    start, target = initial_state[0], observed[0]
    window, tile = lax.axis_index("win"), lax.axis_index("tile")
    lowest = (partner[0] + LANES * tile - 133) % NLON
    offset = lowest % LANES
    case = lowest // LANES + jnp.where(offset >= THIRD, TILES, 0)
    scalars = jnp.stack([offset, (window < WINDOWS - 1).astype(jnp.int32)]).astype(jnp.int32)

    next_low = passed_along(start[: TRACERS // 2], -1)
    west, east, fold, third = call(
        pack_kernel,
        [FIELD, COEFFICIENT, COEFFICIENT, COEFFICIENT],
        [EDGES, EDGES, FOLD, FEW],
        scratch=[(TRACERS + 4, 8, LANES)],
        count=4,
    )(start, mixing, velocity, sea_mask)
    from_east, from_west = around(west, -1), around(east, 1)
    folds = fold_exchange(case, fold, third)
    upper, *folds = lax.optimization_barrier((start[TRACERS // 2 :], *folds))
    next_high = passed_along(upper, -1)
    ends_low, ends_high, spreads, gain, inflow, keep = call(
        forward_kernel,
        [FIELD, COEFFICIENT, COEFFICIENT, COEFFICIENT, EDGES, EDGES, FOLD, FOLD, FEW],
        [PAIR, PAIR, SPREADS, UNFOLDED, UNFOLDED, UNFOLDED],
        scratch=[
            (PLANES, ROWS, LANES),
            (PLANES, ROWS, LANES),
            (2, ROWS, LANES),
            (2, LAT + GHOST, LANES),
            (2, LAT + GHOST, LANES),
        ],
        scalars=True,
        flops=20_000_000,
    )(scalars, start, mixing, velocity, sea_mask, from_west, from_east, *folds)
    forcing, west, east, fold, third = call(
        forcing_kernel,
        [PAIR, PAIR, FIELD, PAIR, PAIR, COEFFICIENT],
        [FIELD, EDGES_FIELDS, EDGES_FIELDS, FOLD_FIELDS, FEW],
        scratch=[(TRACERS + 1, 8, LANES)],
        scalars=True,
        count=4,
    )(scalars, ends_low, ends_high, target, next_low, next_high, sea_mask)
    from_east, from_west = around(west, -1), around(east, 1)
    folds = fold_exchange(case, fold, third)
    ends_low, *folds = lax.optimization_barrier((ends_low, *folds))
    previous_low = passed_along(ends_low, 1)
    gradient, parts = call(
        adjoint_kernel,
        [FIELD, EDGES_FIELDS, EDGES_FIELDS, FOLD_FIELDS, FOLD_FIELDS, FEW, UNFOLDED, UNFOLDED, UNFOLDED, SPREADS]
        + [FIELD, PAIR, PAIR, COEFFICIENT],
        [FIELD, PARTS],
        scratch=[(PLANES, LAT + GHOST, LANES), (PLANES, ROWS, LANES), (PLANES, ROWS, LANES), (2, LAT, LANES)],
        scalars=True,
        flops=20_000_000,
    )(scalars, forcing, from_west, from_east, *folds, gain, inflow, keep, spreads, start, next_low, next_high, sea_mask)
    ends_high, parts = lax.optimization_barrier((ends_high, parts))
    summands = lax.all_to_all(parts, "win", 0, 0, tiled=True)
    previous_high = passed_along(ends_high, 1)
    previous = jnp.concatenate([previous_low, previous_high])
    state_gradient = gradient + jnp.where(window > 0, start - previous, 0.0)
    return state_gradient[None], summands.sum(axis=0)


def solution(mesh):
    in_specs = (
        P("win", None, None, None, "tile"),
        P("win", None, None, None, "tile"),
        P(None, None, "tile"),
        P(None, None, "tile"),
        P(None, None, "tile"),
        P("tile"),
    )
    out_specs = (P("win", None, None, None, "tile"), P(None, "win", "tile"))

    return jax.shard_map(body, mesh=mesh, in_specs=in_specs, out_specs=out_specs, check_vma=False)
```

```python
import functools

import jax
import jax.numpy as jnp
from jax import lax
from jax.experimental import pallas as pl
from jax.experimental.pallas import tpu as pltpu
from jax.sharding import PartitionSpec as P

STEPS = 6
TRACERS = 4
LEVELS = 8
LAT = 64
LANES = 128
NLON = 2048
TILES = NLON // LANES
WINDOWS = 8
HALO = STEPS
GHOST = 8
BLOCKS = (LAT + GHOST) // 8
PAD = 8
ROWS = PAD + LAT + GHOST + PAD
PLANES = TRACERS + 1
STRIP = TRACERS
SEGMENT = 24
SPLIT = 116
THIRD = 117
SLOT = 16


def fold_offset(partner):
    return (partner[0] + LANES * lax.axis_index("tile") + (NLON - 133)) & (LANES - 1)


def onward_factor():
    return (lax.axis_index("win") < WINDOWS - 1).astype(jnp.float32)


def lanes(rows=8):
    return lax.broadcasted_iota(jnp.int32, (rows, LANES), 1)


def moved(rows, shift):
    if isinstance(shift, int):
        shift %= LANES
        if shift == 0:
            return rows
    return pltpu.roll(rows, shift, 1)


def within(lane, first, count):
    return (lane >= first) & (lane < first + count)


def edges_packed(fields, firsts, lane, out):
    west, east = out
    for rows, first in zip(fields, firsts, strict=True):
        here = within(lane, first, HALO)
        west = jnp.where(here, moved(rows, first), west)
        east = jnp.where(here, moved(rows, first + HALO), east)
    return west, east


def field_plane(rows, from_west, first, lane):
    return jnp.where(lane < HALO, moved(from_west, -first), moved(rows, HALO))


def strip_plane(fields, from_east, lane):
    strip = from_east
    for t, rows in enumerate(fields):
        strip = jnp.where(within(lane, SEGMENT * t, 18), moved(rows, SEGMENT * t - 110), strip)
    return jnp.where(lane < SEGMENT * TRACERS, strip, 0.0)


def spread_out(segment, lane):
    segment = jnp.where(lane < SEGMENT, segment, 0.0)
    segment = segment + moved(segment, SEGMENT)
    return segment + moved(segment, 2 * SEGMENT)


def fold_masks(offset):
    lane = lanes(HALO)
    plane = offset + 139 - ((lane + offset + 12) & (LANES - 1)) >= LANES
    strip = offset + 23 - ((lane + offset + 24) & (LANES - 1)) >= LANES
    return lane, plane, strip, lane + THIRD <= offset


def ghost_plane(first, second, third, slot, offset, masks):
    _, plane, _, beyond = masks
    rows = moved(jnp.where(plane, second, first), (offset + 12) & (LANES - 1))
    return jnp.where(beyond, moved(third, (offset + LANES - SLOT * slot) & (LANES - 1)), rows)


def ghost_strip(first, second, t, offset, masks):
    return moved(jnp.where(masks[2], second, first), (offset + SEGMENT * (t + 1)) & (LANES - 1))


def own_columns(plane, strip, t, lane):
    return jnp.where(lane < SPLIT, moved(plane, -HALO), moved(strip, 110 - SEGMENT * t))


def fold_out(values, spare, lane, fold, third, level):
    few = jnp.zeros((8, LANES), jnp.float32)
    for f, rows in enumerate(values):
        back = jnp.take_along_axis(rows, LANES - 1 - lane, axis=1, mode="promise_in_bounds")
        spare[f] = back
        few = jnp.where(within(lane, SLOT * f, 12), moved(back, SLOT * f + 12), few)
    spare[len(values)] = few
    for k in range(HALO):
        for f in range(len(values)):
            fold[level, pl.ds(HALO * f + k, 1), :] = spare[f, pl.ds(7 - k, 1), :]
        third[level, pl.ds(k, 1), :] = spare[len(values), pl.ds(7 - k, 1), :]


def field_slots(group):
    return [SEGMENT * t + 18 - HALO * group for t in range(TRACERS)]


def extra_slots(group):
    return [SEGMENT * f + HALO * group for f in range(3)]


def each_block(count, unrolled, body):
    def several(i, carry):
        for j in range(unrolled):
            body(pl.multiple_of(8 * (unrolled * i + j), 8))
        return carry

    lax.fori_loop(0, count // unrolled, several, 0)


def pack_kernel(init, mixing, velocity, mask, west, east, fold, third, spare):
    lane = lanes()
    third[...] = jnp.zeros_like(third)

    def one_level(level, carry):
        for block in range(LAT // 16):
            out = (jnp.zeros((8, LANES), jnp.float32),) * 2
            for group in range(2):
                rows = pl.ds(8 * (block + LAT // 16 * group), 8)
                wet = mask[level, rows, :].astype(jnp.float32)
                values = [wet * init[t, level, rows, :] for t in range(TRACERS)]
                values += [mixing[level, rows, :], velocity[level, rows, :], wet]
                out = edges_packed(values, field_slots(group) + extra_slots(group), lane, out)
            west[level, pl.ds(8 * block, 8), :], east[level, pl.ds(8 * block, 8), :] = out
        fold_out(values, spare, lane, fold, third, level)
        return carry

    lax.fori_loop(0, mask.shape[0], one_level, 0)


def forward_kernel(
    partner, init, mixing, velocity, mask, from_west, from_east, fold0, fold1, third,
    ends, spreads, gain, inflow, keep, even, odd, wets, counts, drifts,
):
    lane = lanes()
    zero = jnp.zeros((PAD, LANES), jnp.float32)

    @pl.when(pl.program_id(0) == 0)
    def _():
        for at in (pl.ds(0, PAD), pl.ds(PAD + LAT, GHOST), pl.ds(ROWS - PAD, PAD)):
            for plane in range(PLANES):
                even[plane, at, :] = zero
                odd[plane, at, :] = zero
            for plane in range(2):
                wets[plane, at, :] = zero
        for plane in range(2):
            counts[plane, pl.ds(LAT, GHOST), :] = zero
            drifts[plane, pl.ds(LAT, GHOST), :] = zero

    def one_level(level, carry):
        def unfold(row):
            west, east = from_west[level, pl.ds(row, 8), :], from_east[level, pl.ds(row, 8), :]
            for group in range(2):
                rows, to = pl.ds(LAT // 2 * group + row, 8), pl.ds(PAD + LAT // 2 * group + row, 8)
                wet = mask[level, rows, :].astype(jnp.float32)
                fields = [wet * init[t, level, rows, :] for t in range(TRACERS)]
                for t, first in enumerate(field_slots(group)):
                    even[t, to, :] = field_plane(fields[t], west, first, lane)
                even[STRIP, to, :] = strip_plane(fields, moved(east, HALO * group), lane)
                extras = ((mixing[level, rows, :], counts, rows), (velocity[level, rows, :], drifts, rows), (wet, wets, to))
                for (values, target, where), first in zip(extras, extra_slots(group), strict=True):
                    target[0, where, :] = field_plane(values, west, first, lane)
                    segment = jnp.where(lane < 18, moved(values, -110), moved(east, 18 - first))
                    target[1, where, :] = spread_out(segment, lane)

        each_block(LAT // 16, 1, unfold)
        offset = fold_offset(partner)
        masks = fold_masks(offset)
        narrow, few = masks[0], third[level, pl.ds(0, HALO), :]
        rows, to = pl.ds(LAT, HALO), pl.ds(PAD + LAT, HALO)
        strip = jnp.zeros((HALO, LANES), jnp.float32)
        for t in range(TRACERS):
            first, second = (fold[level, pl.ds(HALO * t, HALO), :] for fold in (fold0, fold1))
            even[t, to, :] = ghost_plane(first, second, few, t, offset, masks)
            strip = jnp.where(within(narrow, SEGMENT * t, SEGMENT), ghost_strip(first, second, t, offset, masks), strip)
        even[STRIP, to, :] = strip
        for slot, (target, where) in enumerate(((counts, rows), (drifts, rows), (wets, to)), TRACERS):
            first, second = (fold[level, pl.ds(HALO * slot, HALO), :] for fold in (fold0, fold1))
            target[0, where, :] = ghost_plane(first, second, few, slot, offset, masks)
            target[1, where, :] = spread_out(ghost_strip(first, second, 0, offset, masks), narrow)

        def coefficients(row, own=True):
            rows = pl.ds(row, 8)
            for plane in range(2):
                wet = wets[plane, pl.ds(PAD + row, 8), :]
                west, east = moved(wet, 1), moved(wet, -1)
                north, south = wets[plane, pl.ds(PAD + row + 1, 8), :], wets[plane, pl.ds(PAD + row - 1, 8), :]
                count = (west + east) + (north + south)
                spread = wet * counts[plane, rows, :]
                carried = wet * drifts[plane, rows, :]
                drift = carried * (west if own else east)
                counts[plane, rows, :] = count
                drifts[plane, rows, :] = drift
                gain[plane, level, rows, :] = spread
                inflow[plane, level, rows, :] = spread + carried
                keep[plane, level, rows, :] = 1.0 - (count * spread + drift)

        each_block(LAT // 8, 4, coefficients)
        coefficients(LAT, own=False)

        def step(now, later, moment):
            for block in range(BLOCKS):
                rows, start = pl.ds(8 * block, 8), PAD + 8 * block
                for t in range(PLANES):
                    plane = 1 if t == STRIP else 0
                    centre = now[t, pl.ds(start, 8), :]
                    west, east = moved(centre, 1), moved(centre, -1)
                    spread = (west + east) + (now[t, pl.ds(start + 1, 8), :] + now[t, pl.ds(start - 1, 8), :])
                    spread = spread - counts[plane, rows, :] * centre
                    up = west if block < LAT // 8 else east
                    if block < LAT // 8:
                        spreads[moment, t, level, rows, :] = spread
                    later[t, pl.ds(start, 8), :] = (
                        centre + gain[plane, level, rows, :] * spread + drifts[plane, rows, :] * (up - centre)
                    )

        def two_steps(pair, carry):
            step(even, odd, 2 * pair)
            step(odd, even, 2 * pair + 1)
            return carry

        lax.fori_loop(0, STEPS // 2, two_steps, 0)

        def own_ends(row):
            rows, at = pl.ds(row, 8), pl.ds(PAD + row, 8)
            sea = mask[level, rows, :] > 0
            strip = even[STRIP, at, :]
            for t in range(TRACERS):
                ends[t, level, rows, :] = jnp.where(sea, own_columns(even[t, at, :], strip, t, lane), init[t, level, rows, :])

        each_block(LAT // 8, 2, own_ends)
        return carry

    lax.fori_loop(0, mask.shape[0], one_level, 0)


def forcing_kernel(
    ends, observed, following, mask, forcing, west, east, fold, third, spare
):
    lane = lanes()
    onward = onward_factor()
    third[...] = jnp.zeros_like(third)

    def one_level(level, carry):
        for block in range(LAT // 32):
            out = (jnp.zeros((8, LANES), jnp.float32),) * 2
            for group in range(4):
                rows = pl.ds(8 * (block + LAT // 32 * group), 8)
                wet = mask[level, rows, :].astype(jnp.float32)
                values = []
                for t in range(TRACERS):
                    end = ends[t, level, rows, :]
                    ahead = onward * (end - following[t, level, rows, :])
                    values.append(wet * ((end - observed[t, level, rows, :]) + ahead))
                    forcing[t, level, rows, :] = values[t]
                out = edges_packed(values, field_slots(group), lane, out)
            west[level, pl.ds(8 * block, 8), :], east[level, pl.ds(8 * block, 8), :] = out
        fold_out(values, spare, lane, fold, third, level)
        return carry

    lax.fori_loop(0, mask.shape[0], one_level, 0)


def adjoint_kernel(
    partner, forcing, from_west, from_east, fold0, fold1, third, gain, inflow, keep, spreads, init, following, mask,
    gradient, mixing_part, state, even, odd, sums,
):
    lane = lanes()
    zero = jnp.zeros((PAD, LANES), jnp.float32)
    onward = onward_factor()
    behind = (lax.axis_index("win") > 0).astype(jnp.float32)

    @pl.when(pl.program_id(0) == 0)
    def _():
        for plane in range(PLANES):
            state[plane, pl.ds(LAT, GHOST), :] = zero
            for at in (pl.ds(0, PAD), pl.ds(PAD + LAT, GHOST), pl.ds(ROWS - PAD, PAD)):
                even[plane, at, :] = zero
                odd[plane, at, :] = zero

    def one_level(level, carry):
        def put(plane, row, count, value):
            rows = pl.ds(row, count)
            state[plane, rows, :] = value
            even[plane, pl.ds(PAD + row, count), :] = gain[1 if plane == STRIP else 0, level, rows, :] * value

        def unfold(row):
            west, east = from_west[level, pl.ds(row, 8), :], from_east[level, pl.ds(row, 8), :]
            for group in range(4):
                to = LAT // 4 * group + row
                rows = pl.ds(to, 8)
                fields = [forcing[t, level, rows, :] for t in range(TRACERS)]
                for t, first in enumerate(field_slots(group)):
                    put(t, to, 8, field_plane(fields[t], west, first, lane))
                put(STRIP, to, 8, strip_plane(fields, moved(east, HALO * group), lane))
                sums[0, rows, :] = zero
                sums[1, rows, :] = zero

        each_block(LAT // 32, 1, unfold)
        offset = fold_offset(partner)
        masks = fold_masks(offset)
        narrow, few = masks[0], third[level, pl.ds(0, HALO), :]
        strip = jnp.zeros((HALO, LANES), jnp.float32)
        for t in range(TRACERS):
            first, second = (fold[level, pl.ds(HALO * t, HALO), :] for fold in (fold0, fold1))
            put(t, LAT, HALO, ghost_plane(first, second, few, t, offset, masks))
            strip = jnp.where(within(narrow, SEGMENT * t, SEGMENT), ghost_strip(first, second, t, offset, masks), strip)
        put(STRIP, LAT, HALO, strip)

        def step(now, later, moment):
            for block in range(BLOCKS):
                rows, start = pl.ds(8 * block, 8), PAD + 8 * block
                own = block < LAT // 8
                total = sums[0, rows, :] if own else None
                for t in range(PLANES):
                    plane = 1 if t == STRIP else 0
                    value = state[t, rows, :]
                    passed = now[t, pl.ds(start, 8), :]
                    carried = inflow[plane, level, rows, :] * value
                    west, east = (moved(passed, 1), moved(carried, -1)) if own else (moved(carried, 1), moved(passed, -1))
                    around = (west + east) + (now[t, pl.ds(start + 1, 8), :] + now[t, pl.ds(start - 1, 8), :])
                    if own:
                        product = value * spreads[moment, t, level, rows, :]
                        if t == STRIP:
                            sums[1, rows, :] = sums[1, rows, :] + product
                        else:
                            total = total + product
                    value = keep[plane, level, rows, :] * value + around
                    state[t, rows, :] = value
                    later[t, pl.ds(start, 8), :] = gain[plane, level, rows, :] * value
                if own:
                    sums[0, rows, :] = total

        def two_steps(pair, carry):
            step(even, odd, STEPS - 1 - 2 * pair)
            step(odd, even, STEPS - 2 - 2 * pair)
            return carry

        lax.fori_loop(0, STEPS // 2, two_steps, 0)

        def own_results(row):
            rows = pl.ds(row, 8)
            sea = mask[level, rows, :] > 0
            strip, part = state[STRIP, rows, :], sums[1, rows, :]
            edge = moved(part, 110)
            for t in range(1, TRACERS):
                edge = edge + moved(part, 110 - SEGMENT * t)
            total = jnp.where(lane < SPLIT, moved(sums[0, rows, :], -HALO), edge)
            mixing_part[row // 8, level] = jnp.where(sea, total, 0.0)
            for t in range(TRACERS):
                begun = init[t, level, rows, :]
                land = onward * (begun - following[t, level, rows, :])
                adjoint = jnp.where(sea, own_columns(state[t, rows, :], strip, t, lane), land)
                gradient[t, level, rows, :] = adjoint + behind * begun

        each_block(LAT // 8, 2, own_results)
        return carry

    lax.fori_loop(0, mask.shape[0], one_level, 0)


def spec(shape, dim, count):
    block = tuple(count if i == dim else n for i, n in enumerate(shape))
    return pl.BlockSpec(block, lambda level: tuple(level if i == dim else 0 for i in range(len(shape))))


FIELD = ((TRACERS, LEVELS, LAT, LANES), 1)
COEFFICIENT = ((LEVELS, LAT, LANES), 0)
EDGES = ((LEVELS, LAT // 2, LANES), 0)
EDGES_FIELDS = ((LEVELS, LAT // 4, LANES), 0)
UNFOLDED = ((2, LEVELS, LAT + GHOST, LANES), 1)
SPREADS = ((STEPS, PLANES, LEVELS, LAT, LANES), 2)
PARTS = ((LAT // 8, LEVELS, 8, LANES), 1)
FOLD = ((LEVELS, (TRACERS + 3) * HALO, LANES), 0)
FOLD_FIELDS = ((LEVELS, TRACERS * HALO, LANES), 0)
FEW = ((LEVELS, 8, LANES), 0)
PARTNER = pl.BlockSpec(memory_space=pltpu.SMEM)


def call(kernel, ins, outs, scratch=(), partner=False, flops=0, count=2):
    bytes_accessed = 4 * sum(functools.reduce(lambda a, b: a * b, shape) for shape, _ in (*ins, *outs))
    return pl.pallas_call(
        kernel,
        grid=(LEVELS // count,),
        in_specs=([PARTNER] if partner else []) + [spec(*one, count) for one in ins],
        out_specs=[spec(*one, count) for one in outs],
        out_shape=[jax.ShapeDtypeStruct(shape, jnp.float32) for shape, _ in outs],
        scratch_shapes=[pltpu.VMEM(shape, jnp.float32) for shape in scratch],
        cost_estimate=pl.CostEstimate(flops=flops, bytes_accessed=bytes_accessed, transcendentals=0),
        compiler_params=pltpu.CompilerParams(vmem_limit_bytes=67_000_000),
    )


def passed_along(block, distance):
    return lax.ppermute(block, "win", [(i - distance, i) for i in range(WINDOWS) if i - distance in range(WINDOWS)])


def around(block, steps):
    return lax.ppermute(block, "tile", [(i, (i + steps) % TILES) for i in range(TILES)])


def folded(block, k):
    return lax.ppermute(block, "tile", [(e, (k - e) % TILES) for e in range(TILES)])


def fold_exchange(case, fold, third):
    def branch(k, three):
        def exchange(fold, third):
            few = folded(third, k + 2) if three else jnp.zeros_like(third)
            return folded(fold, k), folded(fold, k + 1), few

        return exchange

    return lax.switch(case, [branch(k, three) for three in (False, True) for k in range(TILES)], fold, third)


def body(initial_state, observed, mixing, velocity, sea_mask, partner):
    start, target = initial_state[0], observed[0]
    lowest = (partner[0] + LANES * lax.axis_index("tile") + (NLON - 133)) & (NLON - 1)
    case = (lowest >> 7) + jnp.where(lowest & (LANES - 1) >= THIRD, TILES, 0)

    west, east, fold, third = call(
        pack_kernel,
        [FIELD, COEFFICIENT, COEFFICIENT, COEFFICIENT],
        [EDGES, EDGES, FOLD, FEW],
        scratch=[(TRACERS + 4, 8, LANES)],
        count=4,
    )(start, mixing, velocity, sea_mask)
    from_east, from_west = around(west, -1), around(east, 1)
    folds = fold_exchange(case, fold, third)
    following = passed_along(start, -1)
    ends, spreads, gain, inflow, keep = call(
        forward_kernel,
        [FIELD, COEFFICIENT, COEFFICIENT, COEFFICIENT, EDGES, EDGES, FOLD, FOLD, FEW],
        [FIELD, SPREADS, UNFOLDED, UNFOLDED, UNFOLDED],
        scratch=[
            (PLANES, ROWS, LANES),
            (PLANES, ROWS, LANES),
            (2, ROWS, LANES),
            (2, LAT + GHOST, LANES),
            (2, LAT + GHOST, LANES),
        ],
        partner=True,
        flops=20_000_000,
    )(partner, start, mixing, velocity, sea_mask, from_west, from_east, *folds)
    forcing, west, east, fold, third = call(
        forcing_kernel,
        [FIELD, FIELD, FIELD, COEFFICIENT],
        [FIELD, EDGES_FIELDS, EDGES_FIELDS, FOLD_FIELDS, FEW],
        scratch=[(TRACERS + 1, 8, LANES)],
        count=4,
    )(ends, target, following, sea_mask)
    from_east, from_west = around(west, -1), around(east, 1)
    folds = fold_exchange(case, fold, third)
    previous = passed_along(ends, 1)
    gradient, parts = call(
        adjoint_kernel,
        [FIELD, EDGES_FIELDS, EDGES_FIELDS, FOLD_FIELDS, FOLD_FIELDS, FEW, UNFOLDED, UNFOLDED, UNFOLDED, SPREADS]
        + [FIELD, FIELD, COEFFICIENT],
        [FIELD, PARTS],
        scratch=[(PLANES, LAT + GHOST, LANES), (PLANES, ROWS, LANES), (PLANES, ROWS, LANES), (2, LAT, LANES)],
        partner=True,
        flops=20_000_000,
    )(partner, forcing, from_west, from_east, *folds, gain, inflow, keep, spreads, start, following, sea_mask)
    summands = lax.all_to_all(parts, "win", 0, 0, tiled=True)
    return (gradient - previous)[None], summands.sum(axis=0)


def solution(mesh):
    in_specs = (
        P("win", None, None, None, "tile"),
        P("win", None, None, None, "tile"),
        P(None, None, "tile"),
        P(None, None, "tile"),
        P(None, None, "tile"),
        P("tile"),
    )
    out_specs = (P("win", None, None, None, "tile"), P(None, "win", "tile"))

    return jax.shard_map(body, mesh=mesh, in_specs=in_specs, out_specs=out_specs, check_vma=False)
```

```python
import functools

import jax
import jax.numpy as jnp
from jax import lax
from jax.experimental import pallas as pl
from jax.experimental.pallas import tpu as pltpu
from jax.sharding import PartitionSpec as P

STEPS = 6
TRACERS = 4
LEVELS = 8
LAT = 64
LANES = 128
NLON = 2048
TILES = NLON // LANES
WINDOWS = 8
HALO = STEPS
GHOST = 8
BLOCKS = (LAT + GHOST) // 8
PAD = 8
ROWS = PAD + LAT + GHOST + PAD
PLANES = TRACERS + 1
STRIP = TRACERS
SEGMENT = 24
SPLIT = 116
THIRD = 117
SLOT = 16


def fold_offset(partner):
    return (partner[0] + LANES * lax.axis_index("tile") + (NLON - 133)) & (LANES - 1)


def onward_factor():
    return (lax.axis_index("win") < WINDOWS - 1).astype(jnp.float32)


def lanes(rows=8):
    return lax.broadcasted_iota(jnp.int32, (rows, LANES), 1)


def moved(rows, shift):
    if isinstance(shift, int):
        shift %= LANES
        if shift == 0:
            return rows
    return pltpu.roll(rows, shift, 1)


def within(lane, first, count):
    return (lane >= first) & (lane < first + count)


def edges_packed(fields, firsts, lane, out):
    west, east = out
    for rows, first in zip(fields, firsts, strict=True):
        here = within(lane, first, HALO)
        west = jnp.where(here, moved(rows, first), west)
        east = jnp.where(here, moved(rows, first + HALO), east)
    return west, east


def field_plane(rows, from_west, first, lane):
    return jnp.where(lane < HALO, moved(from_west, -first), moved(rows, HALO))


def strip_plane(fields, from_east, lane):
    strip = from_east
    for t, rows in enumerate(fields):
        strip = jnp.where(within(lane, SEGMENT * t, 18), moved(rows, SEGMENT * t - 110), strip)
    return jnp.where(lane < SEGMENT * TRACERS, strip, 0.0)


def spread_out(segment, lane):
    segment = jnp.where(lane < SEGMENT, segment, 0.0)
    segment = segment + moved(segment, SEGMENT)
    return segment + moved(segment, 2 * SEGMENT)


def fold_masks(offset):
    lane = lanes(HALO)
    plane = offset + 139 - ((lane + offset + 12) & (LANES - 1)) >= LANES
    strip = offset + 23 - ((lane + offset + 24) & (LANES - 1)) >= LANES
    return lane, plane, strip, lane + THIRD <= offset


def ghost_plane(first, second, third, slot, offset, masks):
    _, plane, _, beyond = masks
    rows = moved(jnp.where(plane, second, first), (offset + 12) & (LANES - 1))
    return jnp.where(beyond, moved(third, (offset + LANES - SLOT * slot) & (LANES - 1)), rows)


def ghost_strip(first, second, t, offset, masks):
    return moved(jnp.where(masks[2], second, first), (offset + SEGMENT * (t + 1)) & (LANES - 1))


def own_columns(plane, strip, t, lane):
    return jnp.where(lane < SPLIT, moved(plane, -HALO), moved(strip, 110 - SEGMENT * t))


def fold_out(values, spare, lane, fold, level):
    few = jnp.zeros((8, LANES), jnp.float32)
    for f, rows in enumerate(values):
        back = jnp.take_along_axis(rows, LANES - 1 - lane, axis=1, mode="promise_in_bounds")
        spare[f] = back
        few = jnp.where(within(lane, SLOT * f, 12), moved(back, SLOT * f + 12), few)
    spare[len(values)] = few
    for k in range(HALO):
        for f in range(len(values) + 1):
            fold[level, pl.ds(HALO * f + k, 1), :] = spare[f, pl.ds(7 - k, 1), :]


def field_slots(group):
    return [SEGMENT * t + 18 - HALO * group for t in range(TRACERS)]


def extra_slots(group):
    return [SEGMENT * f + HALO * group for f in range(3)]


def each_block(count, unrolled, body):
    def several(i, carry):
        for j in range(unrolled):
            body(pl.multiple_of(8 * (unrolled * i + j), 8))
        return carry

    lax.fori_loop(0, count // unrolled, several, 0)


def pack_kernel(init, mixing, velocity, mask, west, east, fold, spare):
    lane = lanes()

    def one_level(level, carry):
        for block in range(LAT // 16):
            out = (jnp.zeros((8, LANES), jnp.float32),) * 2
            for group in range(2):
                rows = pl.ds(8 * (block + LAT // 16 * group), 8)
                wet = mask[level, rows, :].astype(jnp.float32)
                values = [wet * init[t, level, rows, :] for t in range(TRACERS)]
                values += [mixing[level, rows, :], velocity[level, rows, :], wet]
                out = edges_packed(values, field_slots(group) + extra_slots(group), lane, out)
            west[level, pl.ds(8 * block, 8), :], east[level, pl.ds(8 * block, 8), :] = out
        fold_out(values, spare, lane, fold, level)
        return carry

    lax.fori_loop(0, mask.shape[0], one_level, 0)


def forward_kernel(
    partner, init, mixing, velocity, mask, from_west, from_east, fold0, fold1,
    ends, spreads, factors, even, odd, wets, counts, drifts,
):
    lane = lanes()
    zero = jnp.zeros((PAD, LANES), jnp.float32)

    @pl.when(pl.program_id(0) == 0)
    def _():
        for at in (pl.ds(0, PAD), pl.ds(PAD + LAT, GHOST), pl.ds(ROWS - PAD, PAD)):
            for plane in range(PLANES):
                even[plane, at, :] = zero
                odd[plane, at, :] = zero
            for plane in range(2):
                wets[plane, at, :] = zero
        for plane in range(2):
            counts[plane, pl.ds(LAT, GHOST), :] = zero
            drifts[plane, pl.ds(LAT, GHOST), :] = zero

    def one_level(level, carry):
        def unfold(row):
            west, east = from_west[level, pl.ds(row, 8), :], from_east[level, pl.ds(row, 8), :]
            for group in range(2):
                rows, to = pl.ds(LAT // 2 * group + row, 8), pl.ds(PAD + LAT // 2 * group + row, 8)
                wet = mask[level, rows, :].astype(jnp.float32)
                fields = [wet * init[t, level, rows, :] for t in range(TRACERS)]
                for t, first in enumerate(field_slots(group)):
                    even[t, to, :] = field_plane(fields[t], west, first, lane)
                even[STRIP, to, :] = strip_plane(fields, moved(east, HALO * group), lane)
                extras = ((mixing[level, rows, :], counts, rows), (velocity[level, rows, :], drifts, rows), (wet, wets, to))
                for (values, target, where), first in zip(extras, extra_slots(group), strict=True):
                    target[0, where, :] = field_plane(values, west, first, lane)
                    segment = jnp.where(lane < 18, moved(values, -110), moved(east, 18 - first))
                    target[1, where, :] = spread_out(segment, lane)

        each_block(LAT // 16, 1, unfold)
        offset = fold_offset(partner)
        masks = fold_masks(offset)
        narrow, few = masks[0], fold1[level, pl.ds(HALO * (TRACERS + 3), HALO), :]
        rows, to = pl.ds(LAT, HALO), pl.ds(PAD + LAT, HALO)
        strip = jnp.zeros((HALO, LANES), jnp.float32)
        for t in range(TRACERS):
            first, second = (fold[level, pl.ds(HALO * t, HALO), :] for fold in (fold0, fold1))
            even[t, to, :] = ghost_plane(first, second, few, t, offset, masks)
            strip = jnp.where(within(narrow, SEGMENT * t, SEGMENT), ghost_strip(first, second, t, offset, masks), strip)
        even[STRIP, to, :] = strip
        for slot, (target, where) in enumerate(((counts, rows), (drifts, rows), (wets, to)), TRACERS):
            first, second = (fold[level, pl.ds(HALO * slot, HALO), :] for fold in (fold0, fold1))
            target[0, where, :] = ghost_plane(first, second, few, slot, offset, masks)
            target[1, where, :] = spread_out(ghost_strip(first, second, 0, offset, masks), narrow)

        def coefficients(row, own=True):
            rows = pl.ds(row, 8)
            for plane in range(2):
                wet = wets[plane, pl.ds(PAD + row, 8), :]
                west, east = moved(wet, 1), moved(wet, -1)
                north, south = wets[plane, pl.ds(PAD + row + 1, 8), :], wets[plane, pl.ds(PAD + row - 1, 8), :]
                count = (west + east) + (north + south)
                spread = wet * counts[plane, rows, :]
                carried = wet * drifts[plane, rows, :]
                drift = carried * (west if own else east)
                counts[plane, rows, :] = count
                drifts[plane, rows, :] = drift
                factors[level, plane, rows, :] = spread
                factors[level, 2 + plane, rows, :] = spread + carried
                factors[level, 4 + plane, rows, :] = 1.0 - (count * spread + drift)

        each_block(LAT // 8, 4, coefficients)
        coefficients(LAT, own=False)

        def step(now, later, moment):
            for block in range(BLOCKS):
                rows, start = pl.ds(8 * block, 8), PAD + 8 * block
                for t in range(PLANES):
                    plane = 1 if t == STRIP else 0
                    centre = now[t, pl.ds(start, 8), :]
                    west, east = moved(centre, 1), moved(centre, -1)
                    spread = (west + east) + (now[t, pl.ds(start + 1, 8), :] + now[t, pl.ds(start - 1, 8), :])
                    spread = spread - counts[plane, rows, :] * centre
                    up = west if block < LAT // 8 else east
                    if block < LAT // 8:
                        spreads[level, moment, t, rows, :] = spread
                    later[t, pl.ds(start, 8), :] = (
                        centre + factors[level, plane, rows, :] * spread + drifts[plane, rows, :] * (up - centre)
                    )

        def two_steps(pair, carry):
            step(even, odd, 2 * pair)
            step(odd, even, 2 * pair + 1)
            return carry

        lax.fori_loop(0, STEPS // 2, two_steps, 0)

        def own_ends(row):
            rows, at = pl.ds(row, 8), pl.ds(PAD + row, 8)
            sea = mask[level, rows, :] > 0
            strip = even[STRIP, at, :]
            for t in range(TRACERS):
                ends[t, level, rows, :] = jnp.where(sea, own_columns(even[t, at, :], strip, t, lane), init[t, level, rows, :])

        each_block(LAT // 8, 2, own_ends)
        return carry

    lax.fori_loop(0, mask.shape[0], one_level, 0)


def forcing_kernel(
    ends, observed, following, mask, forcing, west, east, fold, spare
):
    lane = lanes()
    onward = onward_factor()

    def one_level(level, carry):
        for block in range(LAT // 32):
            out = (jnp.zeros((8, LANES), jnp.float32),) * 2
            for group in range(4):
                rows = pl.ds(8 * (block + LAT // 32 * group), 8)
                wet = mask[level, rows, :].astype(jnp.float32)
                values = []
                for t in range(TRACERS):
                    end = ends[t, level, rows, :]
                    ahead = onward * (end - following[t, level, rows, :])
                    values.append(wet * ((end - observed[t, level, rows, :]) + ahead))
                    forcing[t, level, rows, :] = values[t]
                out = edges_packed(values, field_slots(group), lane, out)
            west[level, pl.ds(8 * block, 8), :], east[level, pl.ds(8 * block, 8), :] = out
        fold_out(values, spare, lane, fold, level)
        return carry

    lax.fori_loop(0, mask.shape[0], one_level, 0)


def adjoint_kernel(
    partner, forcing, from_west, from_east, fold0, fold1, factors, spreads, init, following, mask,
    gradient, mixing_part, state, even, odd, sums,
):
    lane = lanes()
    zero = jnp.zeros((PAD, LANES), jnp.float32)
    onward = onward_factor()
    behind = (lax.axis_index("win") > 0).astype(jnp.float32)

    @pl.when(pl.program_id(0) == 0)
    def _():
        for plane in range(PLANES):
            state[plane, pl.ds(LAT, GHOST), :] = zero
            for at in (pl.ds(0, PAD), pl.ds(PAD + LAT, GHOST), pl.ds(ROWS - PAD, PAD)):
                even[plane, at, :] = zero
                odd[plane, at, :] = zero

    def one_level(level, carry):
        def put(plane, row, count, value):
            rows = pl.ds(row, count)
            state[plane, rows, :] = value
            even[plane, pl.ds(PAD + row, count), :] = factors[level, 1 if plane == STRIP else 0, rows, :] * value

        def unfold(row):
            west, east = from_west[level, pl.ds(row, 8), :], from_east[level, pl.ds(row, 8), :]
            for group in range(4):
                to = LAT // 4 * group + row
                rows = pl.ds(to, 8)
                fields = [forcing[t, level, rows, :] for t in range(TRACERS)]
                for t, first in enumerate(field_slots(group)):
                    put(t, to, 8, field_plane(fields[t], west, first, lane))
                put(STRIP, to, 8, strip_plane(fields, moved(east, HALO * group), lane))
                sums[0, rows, :] = zero
                sums[1, rows, :] = zero

        each_block(LAT // 32, 1, unfold)
        offset = fold_offset(partner)
        masks = fold_masks(offset)
        narrow, few = masks[0], fold1[level, pl.ds(HALO * TRACERS, HALO), :]
        strip = jnp.zeros((HALO, LANES), jnp.float32)
        for t in range(TRACERS):
            first, second = (fold[level, pl.ds(HALO * t, HALO), :] for fold in (fold0, fold1))
            put(t, LAT, HALO, ghost_plane(first, second, few, t, offset, masks))
            strip = jnp.where(within(narrow, SEGMENT * t, SEGMENT), ghost_strip(first, second, t, offset, masks), strip)
        put(STRIP, LAT, HALO, strip)

        def step(now, later, moment):
            for block in range(BLOCKS):
                rows, start = pl.ds(8 * block, 8), PAD + 8 * block
                own = block < LAT // 8
                total = sums[0, rows, :] if own else None
                for t in range(PLANES):
                    plane = 1 if t == STRIP else 0
                    value = state[t, rows, :]
                    passed = now[t, pl.ds(start, 8), :]
                    carried = factors[level, 2 + plane, rows, :] * value
                    west, east = (moved(passed, 1), moved(carried, -1)) if own else (moved(carried, 1), moved(passed, -1))
                    around = (west + east) + (now[t, pl.ds(start + 1, 8), :] + now[t, pl.ds(start - 1, 8), :])
                    if own:
                        product = value * spreads[level, moment, t, rows, :]
                        if t == STRIP:
                            sums[1, rows, :] = sums[1, rows, :] + product
                        else:
                            total = total + product
                    value = factors[level, 4 + plane, rows, :] * value + around
                    state[t, rows, :] = value
                    later[t, pl.ds(start, 8), :] = factors[level, plane, rows, :] * value
                if own:
                    sums[0, rows, :] = total

        def two_steps(pair, carry):
            step(even, odd, STEPS - 1 - 2 * pair)
            step(odd, even, STEPS - 2 - 2 * pair)
            return carry

        lax.fori_loop(0, STEPS // 2, two_steps, 0)

        def own_results(row):
            rows = pl.ds(row, 8)
            sea = mask[level, rows, :] > 0
            strip, part = state[STRIP, rows, :], sums[1, rows, :]
            edge = moved(part, 110)
            for t in range(1, TRACERS):
                edge = edge + moved(part, 110 - SEGMENT * t)
            total = jnp.where(lane < SPLIT, moved(sums[0, rows, :], -HALO), edge)
            mixing_part[row // 8, level] = jnp.where(sea, total, 0.0)
            for t in range(TRACERS):
                begun = init[t, level, rows, :]
                land = onward * (begun - following[t, level, rows, :])
                adjoint = jnp.where(sea, own_columns(state[t, rows, :], strip, t, lane), land)
                gradient[t, level, rows, :] = adjoint + behind * begun

        each_block(LAT // 8, 2, own_results)
        return carry

    lax.fori_loop(0, mask.shape[0], one_level, 0)


def spec(shape, dim, count):
    block = tuple(count if i == dim else n for i, n in enumerate(shape))
    return pl.BlockSpec(block, lambda level: tuple(level if i == dim else 0 for i in range(len(shape))))


FIELD = ((TRACERS, LEVELS, LAT, LANES), 1)
COEFFICIENT = ((LEVELS, LAT, LANES), 0)
EDGES = ((LEVELS, LAT // 2, LANES), 0)
EDGES_FIELDS = ((LEVELS, LAT // 4, LANES), 0)
FACTORS = ((LEVELS, 6, LAT + GHOST, LANES), 0)
SPREADS = ((LEVELS, STEPS, PLANES, LAT, LANES), 0)
PARTS = ((LAT // 8, LEVELS, 8, LANES), 1)
FOLD = ((LEVELS, (TRACERS + 4) * HALO, LANES), 0)
FOLD_FIELDS = ((LEVELS, (TRACERS + 1) * HALO, LANES), 0)
PARTNER = pl.BlockSpec(memory_space=pltpu.SMEM)


def call(kernel, ins, outs, scratch=(), partner=False, flops=0, count=1):
    bytes_accessed = 4 * sum(functools.reduce(lambda a, b: a * b, shape) for shape, _ in (*ins, *outs))
    return pl.pallas_call(
        kernel,
        grid=(LEVELS // count,),
        in_specs=([PARTNER] if partner else []) + [spec(*one, count) for one in ins],
        out_specs=[spec(*one, count) for one in outs],
        out_shape=[jax.ShapeDtypeStruct(shape, jnp.float32) for shape, _ in outs],
        scratch_shapes=[pltpu.VMEM(shape, jnp.float32) for shape in scratch],
        cost_estimate=pl.CostEstimate(flops=flops, bytes_accessed=bytes_accessed, transcendentals=0),
        compiler_params=pltpu.CompilerParams(vmem_limit_bytes=67_000_000),
    )


def passed_along(block, distance):
    return lax.ppermute(block, "win", [(i - distance, i) for i in range(WINDOWS) if i - distance in range(WINDOWS)])


def around(block, steps):
    return lax.ppermute(block, "tile", [(i, (i + steps) % TILES) for i in range(TILES)])


def folded(block, k):
    return lax.ppermute(block, "tile", [(e, (k - e) % TILES) for e in range(TILES)])


def fold_exchange(case, fold):
    def branch(k, three):
        def exchange(fold):
            first, second = folded(fold, k), folded(fold, k + 1)
            if three:
                few = folded(fold[:, -HALO:], k + 2)
                second = jnp.concatenate([second[:, :-HALO], few], axis=1)
            return first, second

        return exchange

    return lax.switch(case, [branch(k, three) for three in (False, True) for k in range(TILES)], fold)


def body(initial_state, observed, mixing, velocity, sea_mask, partner):
    start, target = initial_state[0], observed[0]
    lowest = (partner[0] + LANES * lax.axis_index("tile") + (NLON - 133)) & (NLON - 1)
    case = (lowest >> 7) + jnp.where(lowest & (LANES - 1) >= THIRD, TILES, 0)

    west, east, fold = call(
        pack_kernel,
        [FIELD, COEFFICIENT, COEFFICIENT, COEFFICIENT],
        [EDGES, EDGES, FOLD],
        scratch=[(TRACERS + 4, 8, LANES)],
        count=4,
    )(start, mixing, velocity, sea_mask)
    from_east, from_west = around(west, -1), around(east, 1)
    folds = fold_exchange(case, fold)
    following = passed_along(start, -1)
    ends, spreads, factors = call(
        forward_kernel,
        [FIELD, COEFFICIENT, COEFFICIENT, COEFFICIENT, EDGES, EDGES, FOLD, FOLD],
        [FIELD, SPREADS, FACTORS],
        scratch=[
            (PLANES, ROWS, LANES),
            (PLANES, ROWS, LANES),
            (2, ROWS, LANES),
            (2, LAT + GHOST, LANES),
            (2, LAT + GHOST, LANES),
        ],
        partner=True,
        flops=20_000_000,
    )(partner, start, mixing, velocity, sea_mask, from_west, from_east, *folds)
    forcing, west, east, fold = call(
        forcing_kernel,
        [FIELD, FIELD, FIELD, COEFFICIENT],
        [FIELD, EDGES_FIELDS, EDGES_FIELDS, FOLD_FIELDS],
        scratch=[(TRACERS + 1, 8, LANES)],
        count=4,
    )(ends, target, following, sea_mask)
    from_east, from_west = around(west, -1), around(east, 1)
    folds = fold_exchange(case, fold)
    previous = passed_along(ends, 1)
    gradient, parts = call(
        adjoint_kernel,
        [FIELD, EDGES_FIELDS, EDGES_FIELDS, FOLD_FIELDS, FOLD_FIELDS, FACTORS, SPREADS, FIELD, FIELD]
        + [COEFFICIENT],
        [FIELD, PARTS],
        scratch=[(PLANES, LAT + GHOST, LANES), (PLANES, ROWS, LANES), (PLANES, ROWS, LANES), (2, LAT, LANES)],
        partner=True,
        flops=20_000_000,
    )(partner, forcing, from_west, from_east, *folds, factors, spreads, start, following, sea_mask)
    summands = lax.all_to_all(parts, "win", 0, 0, tiled=True)
    state_gradient = (gradient - previous)[None]
    return state_gradient, summands.sum(axis=0)


def solution(mesh):
    in_specs = (
        P("win", None, None, None, "tile"),
        P("win", None, None, None, "tile"),
        P(None, None, "tile"),
        P(None, None, "tile"),
        P(None, None, "tile"),
        P("tile"),
    )
    out_specs = (P("win", None, None, None, "tile"), P(None, "win", "tile"))

    return jax.shard_map(body, mesh=mesh, in_specs=in_specs, out_specs=out_specs, check_vma=False)
```
